512 devices in a mesh: frame: 16 (over z), dom: 8 (over x, core), coef: 4 (over y).
Axes of the slice: x: 4, y: 4, z: 16, core: 2. Of those that a mesh axis runs over, the one named last changes fastest.
Arguments:
- geometry: float32 [32, 524288], P('coef', ('frame', 'dom')), may hold values from -1 to 1
- fraction: float32 [32, 524288], P('coef', ('frame', 'dom')), may hold values from 0 to 1
- interval: int32 [32, 524288], P('coef', ('frame', 'dom')), may hold values from 0 to 156
- pattern: int32 [32, 4096], P('coef', ('frame', 'dom')), may hold values from 0 to 95
- target: float32 [524288], P(('frame', 'dom')), may hold values from -8 to 8
Outputs:
- solution: float32 [384, 160], P('coef')
- residual: float32 [524288], P(('frame', 'dom'))
The draws below stay inside these ranges and needn't reach their ends.
Inputs may be any that keep to these rules, and one draw needn't show every extreme that they name: The spline of a slot reads coefficients interval to interval + 3 of its type. Slot s refers to pair type (s // 8) * 96 + pattern.
All inputs are finite; a program needn't handle non-finite values.
Results may differ from the reference program's by a relative error of at most 0.0003.
Values sent between devices are 32-bit elements; how exact they have to be, the bound alone decides.
No kernel may reach another device: no remote copies, remote signals or barrier semaphores. Data moves between devices by JAX's collectives and lax.ppermute only.
A program may use at most 64 MiB of HBM per device.

```python
import jax
import jax.numpy as jnp
from jax import lax

NK = 160
TYPES = 384
NB = 8
ITERS = 2
ROWS = 524288
SLOTS = 32
TILES = 4096
TYPES_DEV = 96
N_COEF = 4


def place_ends(values, own_key, low, largest):
    index_at = [jax.random.randint(jax.random.fold_in(own_key, axis), (), 0, length) for axis, length in enumerate(values.shape)]
    widest = values.shape.index(max(values.shape))
    next_to = index_at[:widest] + [(index_at[widest] + 1) % values.shape[widest]] + index_at[widest + 1:]
    return values.at[tuple(index_at)].set(low).at[tuple(next_to)].set(largest)


def level_of(stream_key, shape, shards, low, high):
    gain = 1.0
    for axis_at, parts in shards:
        draws = jax.random.uniform(jax.random.fold_in(jax.random.fold_in(stream_key, 6), axis_at), (parts,), jnp.float32, low / len(shards), high / len(shards))
        gain = gain * jnp.repeat(jnp.exp(draws), shape[axis_at] // parts).reshape((-1,) + (1,) * (len(shape) - 1 - axis_at))
    return gain


def scatter_about(own_key, dims, spread, most, cuts=(), kind=jnp.bfloat16):
    result = spread * jax.random.normal(own_key, dims, jnp.float32)
    if cuts:
        result = result * level_of(own_key, dims, cuts, -0.22, 0.18)
    return jnp.clip(result, -most, most).astype(kind)


def setup_inputs(seed: int = 0) -> dict:
    streams_of = jax.random.split(jax.random.key(seed), 6)
    geometry = jnp.clip(jax.random.uniform(streams_of[0], (SLOTS, ROWS), jnp.float32, -1.0, 1.0) * level_of(streams_of[0], (SLOTS, ROWS), ((0, 4), (1, 128)), -0.4, 0.0), -1.0, 1.0)
    fraction = jnp.clip(1.0 * jax.random.uniform(streams_of[1], (SLOTS, ROWS), jnp.float32) ** level_of(streams_of[1], (SLOTS, ROWS), ((0, 4), (1, 128)), -0.2, 0.2), 0.0, 1.0)
    interval = place_ends(jax.random.randint(streams_of[2], (SLOTS, ROWS), 0, NK - 3), jax.random.fold_in(streams_of[2], 1), 0, (NK - 3) - 1).astype(jnp.int32)
    pattern = place_ends(jax.random.randint(streams_of[3], (SLOTS, TILES), 0, TYPES_DEV), jax.random.fold_in(streams_of[3], 1), 0, TYPES_DEV - 1).astype(jnp.int32)
    target = scatter_about(streams_of[4], (ROWS,), 1.0, 8.0, ((0, 128),), jnp.float32)
    return dict(geometry=geometry, fraction=fraction, interval=interval, pattern=pattern, target=target)


def spline_weights(fraction):
    square = fraction * fraction
    cube = square * fraction
    return ((1.0 - fraction) ** 3 / 6.0, (3.0 * cube - 6.0 * square + 4.0) / 6.0,
            (-3.0 * cube + 3.0 * square + 3.0 * fraction + 1.0) / 6.0, cube / 6.0)


def reference(geometry, fraction, interval, pattern, target):
    per_coef = TYPES // N_COEF
    slot_ids = jnp.arange(SLOTS, dtype=jnp.int32)
    kinds = ((slot_ids // NB) * per_coef).astype(jnp.int32)[:, None] + pattern

    def slot_data(slot):
        row_kind = jnp.repeat(kinds[slot], 128)
        base = (row_kind * NK + interval[slot]).astype(jnp.int32)
        weights = spline_weights(fraction[slot])
        return base, weights, geometry[slot]

    def forward(flat):
        def step(image, slot):
            base, weights, geom = slot_data(slot)
            value = jnp.zeros((ROWS,), jnp.float32)
            for offset in range(4):
                value = value + weights[offset] * flat[base + offset]
            return image + geom * value, None
        image, _ = lax.scan(step, jnp.zeros((ROWS,), jnp.float32), slot_ids)
        return image

    def backward(resid):
        def step(total, slot):
            base, weights, geom = slot_data(slot)
            for offset in range(4):
                total = total.at[base + offset].add(geom * weights[offset] * resid)
            return total, None
        total, _ = lax.scan(step, jnp.zeros((TYPES * NK,), jnp.float32), slot_ids)
        return total

    residual = target
    gradient = backward(residual)
    gamma = jnp.sum(gradient * gradient)
    direction = gradient
    solution = jnp.zeros_like(gradient)
    for step_index in range(ITERS):
        image = forward(direction)
        alpha = gamma / jnp.sum(image * image)
        solution = solution + alpha * direction
        residual = residual - alpha * image
        if step_index + 1 < ITERS:
            gradient = backward(residual)
            gamma_next = jnp.sum(gradient * gradient)
            direction = gradient + (gamma_next / gamma) * direction
            gamma = gamma_next
    return solution.reshape(TYPES, NK), residual
```

```python
import functools

import jax
import jax.numpy as jnp
from jax import lax
from jax.experimental import pallas as pl
from jax.experimental.pallas import tpu as pltpu
from jax.sharding import PartitionSpec as P

NK = 160
TYPES = 384
TD = 96
HIGH = 24
KNOTS = TD + HIGH
TABLE = 128
PAIRS = 256
IMAGE = 40

VMEM = pl.BlockSpec(memory_space=pltpu.VMEM)
F32 = jnp.float32
BF16 = jnp.bfloat16


def call(kernel, name, *shapes):
    outs = [jax.ShapeDtypeStruct(s, F32) for s in shapes]
    return functools.partial(_run, kernel, name, outs)


def _run(kernel, name, outs, *args, scratch=()):
    return pl.pallas_call(
        kernel,
        out_shape=outs,
        in_specs=[VMEM] * len(args),
        out_specs=[VMEM] * len(outs),
        scratch_shapes=list(scratch),
        name=name,
    )(*args)


def split(value):
    high = value.astype(BF16)
    return high, (value - high.astype(F32)).astype(BF16)


def total_of(value):
    return jnp.sum(jnp.sum(value, axis=0, keepdims=True), axis=1, keepdims=True)


def parts_sum(ref, count, rows):
    total = ref[0:rows, :]
    for at in range(1, count):
        total = total + ref[at * rows : (at + 1) * rows, :]
    return total


def weights(u):
    square = u * u
    cube = square * u
    rest = 1.0 - u
    return (
        rest * rest * rest * (1.0 / 6.0),
        (3.0 * cube - 6.0 * square + 4.0) * (1.0 / 6.0),
        (-3.0 * cube + 3.0 * square + 3.0 * u + 1.0) * (1.0 / 6.0),
        cube * (1.0 / 6.0),
    )


POWERS = (
    (1.0 / 6.0, -0.5, 0.5, -1.0 / 6.0),
    (2.0 / 3.0, 0.0, -1.0, 0.5),
    (1.0 / 6.0, 0.5, 0.5, -0.5),
    (0.0, 0.0, 0.0, 1.0 / 6.0),
)


def power_rows(first):
    sub = lax.broadcasted_iota(jnp.int32, (8, 128), 0)
    out = []
    for power in range(4):
        row = jnp.zeros((8, 128), F32)
        for j in range(4):
            if POWERS[j][power]:
                row = jnp.where(sub == first + j, POWERS[j][power], row)
        out.append(row)
    return out


def transposed(geom_ref, frac_ref, knot_ref, patt_ref, resid_ref, total, out_ref, parts_ref, tops_ref, tile_count):
    knots = lax.broadcasted_iota(jnp.int32, (NK // 16, 16, 128), 0) * 16 + lax.broadcasted_iota(
        jnp.int32, (NK // 16, 16, 128), 1
    )
    knots = knots.astype(F32).astype(BF16)
    one, zero = jnp.ones((), BF16), jnp.zeros((), BF16)
    powers = (power_rows(0), power_rows(4))

    def tile(t, _):
        lanes = pl.ds(pl.multiple_of(t * 128, 128), 128)
        amount = geom_ref[:, lanes] * resid_ref[pl.ds(t, 1), :]
        frac = frac_ref[:, lanes]
        knot = knot_ref[:, lanes].astype(F32)
        for pair in range(4):
            values, hits = [], []
            for half in range(2):
                s = 2 * pair + half
                p0, p1, p2, p3 = powers[half]
                u = jnp.broadcast_to(frac[s : s + 1, :], (8, 128))
                a = jnp.broadcast_to(amount[s : s + 1, :], (8, 128))
                values.append(a * (p0 + u * (p1 + u * (p2 + u * p3))))
                at = jnp.broadcast_to(knot[s : s + 1, :], (16, 128)).astype(BF16)
                hits.append(jnp.where(knots == at[None], one, zero).reshape(NK, 128))
            value = jnp.concatenate(values, axis=1)
            rounded = value.astype(BF16).astype(F32)
            left = jnp.concatenate([rounded, value - rounded], axis=0).astype(BF16)
            got = lax.dot_general(
                left, jnp.concatenate(hits, axis=1), (((1,), (1,)), ((), ())), preferred_element_type=F32
            )
            rows = pl.ds(pl.multiple_of((t * 4 + pair) * 8, 8), 8)
            got = got[0:8, :] + got[8:16, :]
            parts_ref[rows, :] = got[:, 0:128]
            tops_ref[rows, 0 : NK - 128] = got[:, 128:NK]
        return 0

    tops_ref[...] = jnp.zeros((4 * PAIRS, 128), F32)
    lax.fori_loop(0, tile_count, tile, 0)

    lane = lax.broadcasted_iota(jnp.int32, (8, 128), 1)
    picks = jnp.concatenate(
        [jnp.where(lane == patt_ref[:, t : t + 1], 1.0, 0.0) for t in range(tile_count)], axis=0
    )
    picks = jnp.transpose(picks).astype(BF16)[0:TD, :]
    grad = None
    for j in range(4):
        rows = pl.ds(j, PAIRS, stride=4)
        piece = jnp.concatenate([parts_ref[rows, :], tops_ref[rows, :]], axis=1)
        high, low = split(piece)
        got = jnp.dot(picks, high, preferred_element_type=F32) + jnp.dot(picks, low, preferred_element_type=F32)
        grad = got if j == 0 else grad + pltpu.roll(got, j, 1)
    out_ref[0:TD, :] = grad[:, 0:128]
    top = grad[:, 128:256]
    packed = top[0:HIGH]
    for q in range(1, 4):
        packed = packed + pltpu.roll(top[q * HIGH : (q + 1) * HIGH], 32 * q, 1)
    out_ref[TD:KNOTS, :] = packed
    sub = lax.broadcasted_iota(jnp.int32, (8, 128), 0)
    out_ref[KNOTS:TABLE, :] = jnp.where(sub == 0, total, 0.0)


def applied(geom_ref, frac_ref, knot_ref, patt_ref, table, out_ref, chosen_ref, tile_count):
    lane = lax.broadcasted_iota(jnp.int32, (8, 128), 1)
    low_rows, high_rows, shifts = [], [], []
    for t in range(tile_count):
        kind = jnp.broadcast_to(patt_ref[:, t : t + 1], (8, 128))
        block = jnp.where(kind >= HIGH, 1, 0) + jnp.where(kind >= 2 * HIGH, 1, 0) + jnp.where(kind >= 3 * HIGH, 1, 0)
        low_rows.append(jnp.where(lane == kind, 1.0, 0.0))
        high_rows.append(jnp.where(lane == TD + kind - HIGH * block, 1.0, 0.0))
        shifts.append(32 * block)
    picks = jnp.concatenate(low_rows + high_rows, axis=0).astype(BF16)
    high, low = split(table)
    chosen_ref[...] = jnp.dot(picks, high, preferred_element_type=F32) + jnp.dot(
        picks, low, preferred_element_type=F32
    )
    for t in range(tile_count):
        lanes = slice(128 * t, 128 * (t + 1))
        base = knot_ref[:, lanes]
        first = chosen_ref[8 * t : 8 * t + 8, :]
        last = chosen_ref[PAIRS + 8 * t : PAIRS + 8 * t + 8, :]
        value = None
        for j, weight in enumerate(weights(frac_ref[:, lanes])):
            at = base + j
            near = jnp.take_along_axis(first, at & 127, axis=1, mode="promise_in_bounds")
            far = jnp.take_along_axis(last, (at & 31) + shifts[t], axis=1, mode="promise_in_bounds")
            term = weight * jnp.where(at >= 128, far, near)
            value = term if j == 0 else value + term
        row = jnp.sum(geom_ref[:, lanes] * value, axis=0, keepdims=True)
        for c in range(out_ref.shape[0] // IMAGE):
            out_ref[c * IMAGE + t : c * IMAGE + t + 1, :] = row
    gamma = jnp.broadcast_to(total_of(table[0:KNOTS] * table[0:KNOTS]), (8, 128))
    for c in range(out_ref.shape[0] // IMAGE):
        out_ref[c * IMAGE + 32 : (c + 1) * IMAGE, :] = gamma


def first_back(geom, frac, knot, patt, resid, out, parts, tops):
    transposed(geom, frac, knot, patt, resid, 0.0, out, parts, tops, 32)


def later_back(geom, frac, knot, patt, got, out, image, gamma, parts, tops):
    whole = parts_sum(got, got.shape[0] // IMAGE, IMAGE)
    image[...] = whole[0:32]
    gamma[...] = whole[32:40]
    total = jnp.broadcast_to(total_of(whole[0:32] * whole[0:32]), (8, 128))
    transposed(geom, frac, knot, patt, image, total, out, parts, tops, 32)


def scattered(count, copies, got, out):
    rows = got.shape[0] // count
    total = parts_sum(got, count, rows)
    for at in range(copies):
        out[at * rows : (at + 1) * rows, :] = total


def first_forward(geom, frac, knot, patt, grad, out, chosen):
    applied(geom, frac, knot, patt, grad[...], out, chosen, 32)


def later_forward(geom, frac, knot, patt, grad, other, gamma, out, table, chosen):
    alpha = gamma[0:1, :] / other[KNOTS : KNOTS + 1, :]
    table[...] = grad[...] - alpha * other[...]
    applied(geom, frac, knot, patt, table[...], out, chosen, 32)


def norm_kernel(got, gamma, image, out, image_out, gamma_out):
    whole = parts_sum(got, got.shape[0] // IMAGE, IMAGE)
    gamma_out[...] = whole[32:40]
    beta = whole[32:33] / gamma[0:1, :]
    result = whole[0:32] + beta * image[...]
    image_out[...] = result
    out[...] = jnp.broadcast_to(total_of(result * result), out.shape)


def last_kernel(got, gamma0, gamma1, grad0, other, grad1, image0, image1, target, sol, resid):
    total1 = jnp.sum(got[...], axis=0, keepdims=True)
    alpha0 = gamma0[0:1, :] / other[KNOTS : KNOTS + 1, :]
    alpha1 = gamma1[0:1, :] / total1
    beta = gamma1[0:1, :] / gamma0[0:1, :]
    resid[...] = target[...] - alpha0 * image0[...] - alpha1 * image1[...]
    table = alpha0 * grad0[...] + alpha1 * (grad1[...] + beta * grad0[...])
    sol[:, 0:128] = table[0:TD]
    packed = table[TD:KNOTS]
    for q in range(4):
        piece = packed if q == 0 else pltpu.roll(packed, 128 - 32 * q, 1)
        sol[q * HIGH : (q + 1) * HIGH, 128:NK] = piece[:, 0:32]


def exchange(value, axis, count):
    rows = value.shape[0]
    got = lax.all_to_all(value.reshape(count, rows * 128 // count), axis, 0, 0, tiled=True)
    return got.reshape(rows, 128)


def on_device(geometry, fraction, interval, pattern, target):
    frames, doms, coefs = lax.axis_size("frame"), lax.axis_size("dom"), lax.axis_size("coef")
    data = (geometry, fraction, interval, pattern)
    target = target.reshape(32, 128)
    piece = TABLE // doms
    parts = [pltpu.VMEM((4 * PAIRS, 128), F32)] * 2
    chosen = [pltpu.VMEM((2 * PAIRS, 128), F32)]

    def reduced(local):
        got = exchange(local, "dom", doms)
        (mine,) = call(functools.partial(scattered, doms, frames), "scatter_dom", (frames * piece, 128))(got)
        got = exchange(mine, "frame", frames)
        (mine,) = call(functools.partial(scattered, frames, doms), "scatter_frame", (TABLE, 128))(got)
        return exchange(mine, "dom", doms)

    (local,) = call(first_back, "back0", (TABLE, 128))(*data, target, scratch=parts)
    grad0 = reduced(local)
    (local,) = call(first_forward, "fwd0", (coefs * IMAGE, 128))(*data, grad0, scratch=chosen)
    got = exchange(local, "coef", coefs)
    local, image0, gamma0 = call(later_back, "back1", (TABLE, 128), (32, 128), (8, 128))(*data, got, scratch=parts)
    other = reduced(local)
    local, grad1 = call(later_forward, "fwd1", (coefs * IMAGE, 128), (TABLE, 128))(
        *data, grad0, other, gamma0, scratch=chosen
    )
    got = exchange(local, "coef", coefs)
    local, image1, gamma1 = call(norm_kernel, "norm", (frames * doms, 128), (32, 128), (8, 128))(got, gamma0, image0)
    got = exchange(local, ("frame", "dom"), frames * doms)
    sol, resid = call(last_kernel, "last", (TD, NK), (32, 128))(
        got, gamma0, gamma1, grad0, other, grad1, image0, image1, target
    )
    return sol, resid.reshape(4096)


def solution(mesh):
    in_specs = (
        P("coef", ("frame", "dom")),
        P("coef", ("frame", "dom")),
        P("coef", ("frame", "dom")),
        P("coef", ("frame", "dom")),
        P(("frame", "dom")),
    )
    out_specs = (P("coef", None), P(("frame", "dom")))
    return jax.shard_map(on_device, mesh=mesh, in_specs=in_specs, out_specs=out_specs, check_vma=False)
```

```python
import functools

import jax
import jax.numpy as jnp
from jax import lax
from jax.experimental import pallas as pl
from jax.experimental.pallas import tpu as pltpu
from jax.sharding import PartitionSpec as P

NK = 160
TYPES = 384
TD = 96
HIGH = 24
KNOTS = TD + HIGH
TABLE = 128
PAIRS = 256
IMAGE = 40
UNROLL = 4

VMEM = pl.BlockSpec(memory_space=pltpu.VMEM)
F32 = jnp.float32
BF16 = jnp.bfloat16


def call(kernel, name, *shapes):
    outs = [jax.ShapeDtypeStruct(s, F32) for s in shapes]
    return functools.partial(_run, kernel, name, outs)


def _run(kernel, name, outs, *args, scratch=()):
    return pl.pallas_call(
        kernel,
        out_shape=outs,
        in_specs=[VMEM] * len(args),
        out_specs=[VMEM] * len(outs),
        scratch_shapes=list(scratch),
        name=name,
        compiler_params=pltpu.CompilerParams(vmem_limit_bytes=8 << 20),
    )(*args)


def split(value):
    high = value.astype(BF16)
    return high, (value - high.astype(F32)).astype(BF16)


def total_of(value):
    return jnp.sum(jnp.sum(value, axis=0, keepdims=True), axis=1, keepdims=True)


def parts_sum(ref, count, rows):
    total = ref[0:rows, :]
    for at in range(1, count):
        total = total + ref[at * rows : (at + 1) * rows, :]
    return total


def weights(u):
    square = u * u
    cube = square * u
    rest = 1.0 - u
    return (
        rest * rest * rest * (1.0 / 6.0),
        (3.0 * cube - 6.0 * square + 4.0) * (1.0 / 6.0),
        (-3.0 * cube + 3.0 * square + 3.0 * u + 1.0) * (1.0 / 6.0),
        cube * (1.0 / 6.0),
    )


POWERS = (
    (1.0 / 6.0, -0.5, 0.5, -1.0 / 6.0),
    (2.0 / 3.0, 0.0, -1.0, 0.5),
    (1.0 / 6.0, 0.5, 0.5, -0.5),
    (0.0, 0.0, 0.0, 1.0 / 6.0),
)


def power_rows(first):
    sub = lax.broadcasted_iota(jnp.int32, (8, 128), 0)
    out = []
    for power in range(4):
        row = jnp.zeros((8, 128), F32)
        for j in range(4):
            if POWERS[j][power]:
                row = jnp.where(sub == first + j, POWERS[j][power], row)
        out.append(row)
    return out


def transposed(geom_ref, frac_ref, knot_ref, patt_ref, resid_ref, total, out_ref, parts_ref, tops_ref, tile_count):
    knots = lax.broadcasted_iota(jnp.int32, (NK // 16, 16, 128), 0) * 16 + lax.broadcasted_iota(
        jnp.int32, (NK // 16, 16, 128), 1
    )
    knots = knots.astype(F32).astype(BF16)
    one, zero = jnp.ones((), BF16), jnp.zeros((), BF16)
    powers = (power_rows(0), power_rows(4))

    def tile(t):
        lanes = pl.ds(pl.multiple_of(t * 128, 128), 128)
        resid = jnp.broadcast_to(resid_ref[pl.ds(t, 1), :], (8, 128))
        for pair in range(4):
            values, hits = [], []
            for half in range(2):
                s = slice(2 * pair + half, 2 * pair + half + 1)
                p0, p1, p2, p3 = powers[half]
                u = jnp.broadcast_to(frac_ref[s, lanes], (8, 128))
                a = jnp.broadcast_to(geom_ref[s, lanes], (8, 128)) * resid
                values.append(a * (p0 + u * (p1 + u * (p2 + u * p3))))
                at = jnp.broadcast_to(knot_ref[s, lanes], (16, 128)).astype(F32).astype(BF16)
                hits.append(jnp.where(knots == at[None], one, zero).reshape(NK, 128))
            value = jnp.concatenate(values, axis=1)
            rounded = value.astype(BF16).astype(F32)
            left = jnp.concatenate([rounded, value - rounded], axis=0).astype(BF16)
            got = lax.dot_general(
                left, jnp.concatenate(hits, axis=1), (((1,), (1,)), ((), ())), preferred_element_type=F32
            )
            rows = pl.ds(pl.multiple_of((t * 4 + pair) * 8, 8), 8)
            got = got[0:8, :] + got[8:16, :]
            parts_ref[rows, :] = got[:, 0:128]
            tops_ref[rows, 0 : NK - 128] = got[:, 128:NK]

    def tiles(step, _):
        for at in range(UNROLL):
            tile(step * UNROLL + at)
        return 0

    tops_ref[...] = jnp.zeros((4 * PAIRS, 128), F32)
    lax.fori_loop(0, tile_count // UNROLL, tiles, 0)

    lane = lax.broadcasted_iota(jnp.int32, (8, 128), 1)
    picks = jnp.concatenate(
        [jnp.where(lane == patt_ref[:, t : t + 1], 1.0, 0.0) for t in range(tile_count)], axis=0
    )
    picks = jnp.transpose(picks).astype(BF16)[0:TD, :]
    grad = None
    for j in range(4):
        rows = pl.ds(j, PAIRS, stride=4)
        piece = jnp.concatenate([parts_ref[rows, :], tops_ref[rows, :]], axis=1)
        high, low = split(piece)
        got = jnp.dot(picks, high, preferred_element_type=F32) + jnp.dot(picks, low, preferred_element_type=F32)
        grad = got if j == 0 else grad + pltpu.roll(got, j, 1)
    out_ref[0:TD, :] = grad[:, 0:128]
    top = grad[:, 128:256]
    packed = top[0:HIGH]
    for q in range(1, 4):
        packed = packed + pltpu.roll(top[q * HIGH : (q + 1) * HIGH], 32 * q, 1)
    out_ref[TD:KNOTS, :] = packed
    sub = lax.broadcasted_iota(jnp.int32, (8, 128), 0)
    out_ref[KNOTS:TABLE, :] = jnp.where(sub == 0, total, 0.0)


def applied(geom_ref, frac_ref, knot_ref, patt_ref, table, out_ref, chosen_ref, tile_count):
    lane = lax.broadcasted_iota(jnp.int32, (8, 128), 1)
    low_rows, high_rows, shifts = [], [], []
    for t in range(tile_count):
        kind = jnp.broadcast_to(patt_ref[:, t : t + 1], (8, 128))
        block = jnp.where(kind >= HIGH, 1, 0) + jnp.where(kind >= 2 * HIGH, 1, 0) + jnp.where(kind >= 3 * HIGH, 1, 0)
        low_rows.append(jnp.where(lane == kind, 1.0, 0.0))
        high_rows.append(jnp.where(lane == TD + kind - HIGH * block, 1.0, 0.0))
        shifts.append(32 * block)
    picks = jnp.concatenate(low_rows + high_rows, axis=0).astype(BF16)
    high, low = split(table)
    chosen_ref[...] = jnp.dot(picks, high, preferred_element_type=F32) + jnp.dot(
        picks, low, preferred_element_type=F32
    )
    for t in range(tile_count):
        lanes = slice(128 * t, 128 * (t + 1))
        base = knot_ref[:, lanes]
        first = chosen_ref[8 * t : 8 * t + 8, :]
        last = chosen_ref[PAIRS + 8 * t : PAIRS + 8 * t + 8, :]
        value = None
        for j, weight in enumerate(weights(frac_ref[:, lanes])):
            at = base + j
            near = jnp.take_along_axis(first, at & 127, axis=1, mode="promise_in_bounds")
            far = jnp.take_along_axis(last, (at & 31) + shifts[t], axis=1, mode="promise_in_bounds")
            term = weight * jnp.where(at >= 128, far, near)
            value = term if j == 0 else value + term
        row = jnp.sum(geom_ref[:, lanes] * value, axis=0, keepdims=True)
        for c in range(out_ref.shape[0] // IMAGE):
            out_ref[c * IMAGE + t : c * IMAGE + t + 1, :] = row
    gamma = jnp.broadcast_to(total_of(table[0:KNOTS] * table[0:KNOTS]), (8, 128))
    for c in range(out_ref.shape[0] // IMAGE):
        out_ref[c * IMAGE + 32 : (c + 1) * IMAGE, :] = gamma


def first_back(geom, frac, knot, patt, resid, out, parts, tops):
    transposed(geom, frac, knot, patt, resid, 0.0, out, parts, tops, 32)


def later_back(geom, frac, knot, patt, got, out, image, gamma, parts, tops):
    whole = parts_sum(got, got.shape[0] // IMAGE, IMAGE)
    image[...] = whole[0:32]
    gamma[...] = whole[32:40]
    total = jnp.broadcast_to(total_of(whole[0:32] * whole[0:32]), (8, 128))
    transposed(geom, frac, knot, patt, image, total, out, parts, tops, 32)


def scattered(count, copies, got, out):
    rows = got.shape[0] // count
    total = parts_sum(got, count, rows)
    for at in range(copies):
        out[at * rows : (at + 1) * rows, :] = total


def first_forward(geom, frac, knot, patt, grad, out, chosen):
    applied(geom, frac, knot, patt, grad[...], out, chosen, 32)


def later_forward(geom, frac, knot, patt, grad, other, gamma, out, table, chosen):
    alpha = gamma[0:1, :] / other[KNOTS : KNOTS + 1, :]
    table[...] = grad[...] - alpha * other[...]
    applied(geom, frac, knot, patt, table[...], out, chosen, 32)


def norm_kernel(got, gamma, image, out, image_out, gamma_out):
    whole = parts_sum(got, got.shape[0] // IMAGE, IMAGE)
    gamma_out[...] = whole[32:40]
    beta = whole[32:33] / gamma[0:1, :]
    result = whole[0:32] + beta * image[...]
    image_out[...] = result
    out[...] = jnp.broadcast_to(total_of(result * result), out.shape)


def last_kernel(got, gamma0, gamma1, grad0, other, grad1, image0, image1, target, sol, resid):
    total1 = jnp.sum(got[...], axis=0, keepdims=True)
    alpha0 = gamma0[0:1, :] / other[KNOTS : KNOTS + 1, :]
    alpha1 = gamma1[0:1, :] / total1
    beta = gamma1[0:1, :] / gamma0[0:1, :]
    resid[...] = target[...] - alpha0 * image0[...] - alpha1 * image1[...]
    table = alpha0 * grad0[...] + alpha1 * (grad1[...] + beta * grad0[...])
    turned = jnp.transpose(table)
    sol[0:128, :] = turned[:, 0:TD]
    lane = lax.broadcasted_iota(jnp.int32, (32, 128), 1)
    top = pltpu.roll(turned[0:32], 128 - TD, 1)
    for q in range(1, 4):
        piece = pltpu.roll(turned[32 * q : 32 * q + 32], (128 - TD + HIGH * q) % 128, 1)
        top = jnp.where(lane >= HIGH * q, piece, top)
    sol[128:NK, :] = top[:, 0:TD]


def exchange(value, axis, count):
    rows = value.shape[0]
    got = lax.all_to_all(value.reshape(count, rows * 128 // count), axis, 0, 0, tiled=True)
    return got.reshape(rows, 128)


def on_device(geometry, fraction, interval, pattern, target):
    frames, doms, coefs = lax.axis_size("frame"), lax.axis_size("dom"), lax.axis_size("coef")
    data = (geometry, fraction, interval, pattern)
    target = target.reshape(32, 128)
    piece = TABLE // doms
    parts = [pltpu.VMEM((4 * PAIRS, 128), F32)] * 2
    chosen = [pltpu.VMEM((2 * PAIRS, 128), F32)]

    def reduced(local):
        got = exchange(local, "dom", doms)
        (mine,) = call(functools.partial(scattered, doms, frames), "scatter_dom", (frames * piece, 128))(got)
        got = exchange(mine, "frame", frames)
        (mine,) = call(functools.partial(scattered, frames, doms), "scatter_frame", (TABLE, 128))(got)
        return exchange(mine, "dom", doms)

    (local,) = call(first_back, "back0", (TABLE, 128))(*data, target, scratch=parts)
    grad0 = reduced(local)
    (local,) = call(first_forward, "fwd0", (coefs * IMAGE, 128))(*data, grad0, scratch=chosen)
    got = exchange(local, "coef", coefs)
    local, image0, gamma0 = call(later_back, "back1", (TABLE, 128), (32, 128), (8, 128))(*data, got, scratch=parts)
    other = reduced(local)
    local, grad1 = call(later_forward, "fwd1", (coefs * IMAGE, 128), (TABLE, 128))(
        *data, grad0, other, gamma0, scratch=chosen
    )
    got = exchange(local, "coef", coefs)
    local, image1, gamma1 = call(norm_kernel, "norm", (frames * doms, 128), (32, 128), (8, 128))(got, gamma0, image0)
    got = exchange(local, ("frame", "dom"), frames * doms)
    sol, resid = call(last_kernel, "last", (NK, TD), (32, 128))(
        got, gamma0, gamma1, grad0, other, grad1, image0, image1, target
    )
    return sol.T, resid.reshape(4096)


def solution(mesh):
    in_specs = (
        P("coef", ("frame", "dom")),
        P("coef", ("frame", "dom")),
        P("coef", ("frame", "dom")),
        P("coef", ("frame", "dom")),
        P(("frame", "dom")),
    )
    out_specs = (P("coef", None), P(("frame", "dom")))
    return jax.shard_map(on_device, mesh=mesh, in_specs=in_specs, out_specs=out_specs, check_vma=False)
```

```python
import functools

import jax
import jax.numpy as jnp
from jax import lax
from jax.experimental import pallas as pl
from jax.experimental.pallas import tpu as pltpu
from jax.sharding import PartitionSpec as P

NK = 160
TYPES = 384
TD = 96
HIGH = 24
KNOTS = TD + HIGH
TABLE = 128
PAIRS = 256
IMAGE = 40
UNROLL = 8
TILES_DEV = 32

VMEM = pl.BlockSpec(memory_space=pltpu.VMEM)
HBM = pl.BlockSpec(memory_space=pltpu.HBM)
F32 = jnp.float32
BF16 = jnp.bfloat16
I32 = jnp.int32


def call(kernel, name, outs, args, scratch=(), space=VMEM):
    outs = [o if isinstance(o, jax.ShapeDtypeStruct) else jax.ShapeDtypeStruct(o, F32) for o in outs]
    return pl.pallas_call(
        kernel,
        out_shape=outs,
        in_specs=[space] * len(args),
        out_specs=[VMEM] * len(outs),
        scratch_shapes=list(scratch),
        name=name,
        compiler_params=pltpu.CompilerParams(vmem_limit_bytes=8 << 20),
    )(*args)


def split(value):
    high = value.astype(BF16)
    return high, (value - high.astype(F32)).astype(BF16)


def total_of(value):
    return jnp.sum(jnp.sum(value, axis=0, keepdims=True), axis=1, keepdims=True)


def parts_sum(ref, count, rows):
    total = ref[0:rows, :]
    for at in range(1, count):
        total = total + ref[at * rows : (at + 1) * rows, :]
    return total


def weights(u):
    square = u * u
    cube = square * u
    rest = 1.0 - u
    return (
        rest * rest * rest * (1.0 / 6.0),
        (3.0 * cube - 6.0 * square + 4.0) * (1.0 / 6.0),
        (-3.0 * cube + 3.0 * square + 3.0 * u + 1.0) * (1.0 / 6.0),
        cube * (1.0 / 6.0),
    )


def prepare(frac_ref, knot_ref, patt_ref, place_ref, high_ref, picks_ref):
    knot = knot_ref[...]
    high = (knot * 205) >> 10
    place_ref[...] = (knot - 5 * high + 1).astype(F32) + frac_ref[...]
    high_ref[...] = high.astype(F32)
    lane = lax.broadcasted_iota(I32, (8, 128), 1)
    picks = [jnp.where(lane == patt_ref[:, t : t + 1], 1.0, 0.0) for t in range(TILES_DEV)]
    picks_ref[...] = jnp.transpose(jnp.concatenate(picks, axis=0))[0:TD, :].astype(BF16)


def transposed(geom_ref, place_ref, high_ref, picks_ref, resid_ref, total, out_ref, parts_ref):
    places = lax.broadcasted_iota(I32, (8, 128), 0).astype(F32)
    rows = lax.broadcasted_iota(I32, (2, 16, 128), 0) * 16 + lax.broadcasted_iota(I32, (2, 16, 128), 1)
    rows = rows.astype(F32).astype(BF16)
    one, zero = jnp.ones((), BF16), jnp.zeros((), BF16)
    empty = jnp.zeros((16, 128), BF16)

    def tile(t):
        lanes = pl.ds(pl.multiple_of(t * 128, 128), 128)
        resid = jnp.broadcast_to(resid_ref[pl.ds(t, 1), :], (8, 128)) * (1.0 / 6.0)
        for pair in range(4):
            values, hits = [], []
            for half in range(2):
                s = slice(2 * pair + half, 2 * pair + half + 1)
                near = jnp.abs(jnp.broadcast_to(place_ref[s, lanes], (8, 128)) - places)
                a = jnp.maximum(2.0 - near, 0.0)
                b = jnp.maximum(1.0 - near, 0.0)
                amount = jnp.broadcast_to(geom_ref[s, lanes], (8, 128)) * resid
                value = amount * (a * a * a - (4.0 * b) * (b * b))
                rounded = value.astype(BF16).astype(F32)
                values.append(jnp.concatenate([rounded, value - rounded], axis=0).astype(BF16))
                at = jnp.broadcast_to(high_ref[s, lanes], (16, 128)).astype(BF16)
                hits.append(jnp.where(rows == at[None], one, zero).reshape(32, 128))
            left = jnp.concatenate(
                [jnp.concatenate([values[0], empty], axis=1), jnp.concatenate([empty, values[1]], axis=1)], axis=0
            )
            got = lax.dot_general(
                left, jnp.concatenate(hits, axis=1), (((1,), (1,)), ((), ())), preferred_element_type=F32
            )
            at = pl.ds(pl.multiple_of((t * 4 + pair) * 16, 16), 16)
            parts_ref[at, 0:32] = jnp.concatenate([got[0:8] + got[8:16], got[16:24] + got[24:32]], axis=0)

    def tiles(step, _):
        for at in range(UNROLL):
            tile(step * UNROLL + at)
        return 0

    lax.fori_loop(0, TILES_DEV // UNROLL, tiles, 0)

    picks = picks_ref[...]
    block = lax.broadcasted_iota(I32, (PAIRS, 128), 1) >> 5
    halves = []
    for group in range(2):
        piece = parts_ref[pl.ds(4 * group, PAIRS, stride=8), :]
        for q in range(1, 4):
            other = pltpu.roll(parts_ref[pl.ds(4 * group + q, PAIRS, stride=8), :], 32 * q, 1)
            piece = jnp.where(block >= q, other, piece)
        halves.append(piece)
    high, low = split(jnp.concatenate(halves, axis=1))
    grad = jnp.dot(picks, high, preferred_element_type=F32) + jnp.dot(picks, low, preferred_element_type=F32)
    source = lax.broadcasted_iota(I32, (256, 256), 0)
    column = lax.broadcasted_iota(I32, (256, 256), 1)
    knot = jnp.where(column >= 128, 128 + (column & 31), column)
    spread = jnp.where(5 * (source & 31) + (source >> 5) == knot, 1.0, 0.0).astype(BF16)
    high, low = split(grad)
    grad = jnp.dot(high, spread, preferred_element_type=F32) + jnp.dot(low, spread, preferred_element_type=F32)
    out_ref[0:TD, :] = grad[:, 0:128]
    packed = grad[0:HIGH, 128:256]
    for q in range(1, 4):
        packed = jnp.where(block[0:HIGH] >= q, grad[q * HIGH : (q + 1) * HIGH, 128:256], packed)
    out_ref[TD:KNOTS, :] = packed
    sub = lax.broadcasted_iota(I32, (8, 128), 0)
    out_ref[KNOTS:TABLE, :] = jnp.where(sub == 0, total, 0.0)


def choose(patt_ref, picks_ref, shift_ref):
    lane = lax.broadcasted_iota(I32, (8, 128), 1)
    low_rows, high_rows = [], []
    for t in range(TILES_DEV):
        kind = jnp.broadcast_to(patt_ref[:, t : t + 1], (8, 128))
        block = jnp.where(kind >= HIGH, 1, 0) + jnp.where(kind >= 2 * HIGH, 1, 0) + jnp.where(kind >= 3 * HIGH, 1, 0)
        low_rows.append(jnp.where(lane == kind, 1.0, 0.0))
        high_rows.append(jnp.where(lane == TD + kind - HIGH * block, 1.0, 0.0))
        shift_ref[8 * t : 8 * t + 8, :] = 32 * block
    picks_ref[...] = jnp.concatenate(low_rows + high_rows, axis=0).astype(BF16)


def applied(geom_ref, frac_ref, knot_ref, picks_ref, shift_ref, table, out_ref, chosen_ref):
    picks = picks_ref[...]
    high, low = split(table)
    chosen_ref[...] = jnp.dot(picks, high, preferred_element_type=F32) + jnp.dot(
        picks, low, preferred_element_type=F32
    )
    for t in range(TILES_DEV):
        lanes = slice(128 * t, 128 * (t + 1))
        slots = slice(8 * t, 8 * t + 8)
        base = knot_ref[:, lanes]
        first = chosen_ref[slots, :]
        last = chosen_ref[PAIRS + 8 * t : PAIRS + 8 * t + 8, :]
        value = None
        for j, weight in enumerate(weights(frac_ref[:, lanes])):
            at = base + j
            near = jnp.take_along_axis(first, at & 127, axis=1, mode="promise_in_bounds")
            far = jnp.take_along_axis(last, (at & 31) + shift_ref[slots, :], axis=1, mode="promise_in_bounds")
            term = weight * jnp.where(at >= 128, far, near)
            value = term if j == 0 else value + term
        row = jnp.sum(geom_ref[:, lanes] * value, axis=0, keepdims=True)
        for c in range(out_ref.shape[0] // IMAGE):
            out_ref[c * IMAGE + t : c * IMAGE + t + 1, :] = row
    gamma = jnp.broadcast_to(total_of(table[0:KNOTS] * table[0:KNOTS]), (8, 128))
    for c in range(out_ref.shape[0] // IMAGE):
        out_ref[c * IMAGE + 32 : (c + 1) * IMAGE, :] = gamma


def first_back(*refs):
    sources, (out, *copies), (place, high, picks), (parts, sems) = refs[:5], refs[5:11], refs[11:14], refs[14:]
    moves = [pltpu.make_async_copy(a, b, sems.at[i]) for i, (a, b) in enumerate(zip(sources, copies, strict=True))]
    for move in moves:
        move.start()
    for move in moves:
        move.wait()
    geom, frac, knot, patt, target = copies
    prepare(frac, knot, patt, place, high, picks)
    transposed(geom, place, high, picks, target, 0.0, out, parts)


def later_back(geom, place, high, picks, got, out, image, gamma, parts):
    whole = parts_sum(got, got.shape[0] // IMAGE, IMAGE)
    image[...] = whole[0:32]
    gamma[...] = whole[32:40]
    total = jnp.broadcast_to(total_of(whole[0:32] * whole[0:32]), (8, 128))
    transposed(geom, place, high, picks, image, total, out, parts)


def scattered(count, copies, got, out):
    rows = got.shape[0] // count
    total = parts_sum(got, count, rows)
    for at in range(copies):
        out[at * rows : (at + 1) * rows, :] = total


def first_forward(geom, frac, knot, patt, grad, out, picks, shift, chosen):
    choose(patt, picks, shift)
    applied(geom, frac, knot, picks, shift, grad[...], out, chosen)


def later_forward(geom, frac, knot, picks, shift, grad, other, gamma, out, table, chosen):
    alpha = gamma[0:1, :] / other[KNOTS : KNOTS + 1, :]
    table[...] = grad[...] - alpha * other[...]
    applied(geom, frac, knot, picks, shift, table[...], out, chosen)


def norm_kernel(got, gamma, image, out, image_out, gamma_out):
    whole = parts_sum(got, got.shape[0] // IMAGE, IMAGE)
    gamma_out[...] = whole[32:40]
    beta = whole[32:33] / gamma[0:1, :]
    result = whole[0:32] + beta * image[...]
    image_out[...] = result
    out[...] = jnp.broadcast_to(total_of(result * result), out.shape)


def last_kernel(got, gamma0, gamma1, grad0, other, grad1, image0, image1, target, sol, resid):
    total1 = jnp.sum(got[...], axis=0, keepdims=True)
    alpha0 = gamma0[0:1, :] / other[KNOTS : KNOTS + 1, :]
    alpha1 = gamma1[0:1, :] / total1
    beta = gamma1[0:1, :] / gamma0[0:1, :]
    resid[...] = target[...] - alpha0 * image0[...] - alpha1 * image1[...]
    table = alpha0 * grad0[...] + alpha1 * (grad1[...] + beta * grad0[...])
    turned = jnp.transpose(table)
    sol[0:128, :] = turned[:, 0:TD]
    lane = lax.broadcasted_iota(I32, (32, 128), 1)
    top = pltpu.roll(turned[0:32], 128 - TD, 1)
    for q in range(1, 4):
        piece = pltpu.roll(turned[32 * q : 32 * q + 32], (128 - TD + HIGH * q) % 128, 1)
        top = jnp.where(lane >= HIGH * q, piece, top)
    sol[128:NK, :] = top[:, 0:TD]


def exchange(value, axis, count):
    rows = value.shape[0]
    got = lax.all_to_all(value.reshape(count, rows * 128 // count), axis, 0, 0, tiled=True)
    return got.reshape(rows, 128)


def on_device(geometry, fraction, interval, pattern, target):
    frames, doms, coefs = lax.axis_size("frame"), lax.axis_size("dom"), lax.axis_size("coef")
    piece = TABLE // doms
    shape = jax.ShapeDtypeStruct
    parts = pltpu.VMEM((8 * PAIRS, 128), F32)
    chosen = pltpu.VMEM((2 * PAIRS, 128), F32)

    def reduced(local):
        got = exchange(local, "dom", doms)
        (mine,) = call(functools.partial(scattered, doms, frames), "scatter_dom", [(frames * piece, 128)], [got])
        got = exchange(mine, "frame", frames)
        (mine,) = call(functools.partial(scattered, frames, doms), "scatter_frame", [(TABLE, 128)], [got])
        return exchange(mine, "dom", doms)

    sources = [geometry, fraction, interval, pattern, target.reshape(32, 128)]
    copies = [shape(s.shape, s.dtype) for s in sources]
    local, geom, frac, knot, patt, target, place, high, types = call(
        first_back,
        "back0",
        [(TABLE, 128), *copies, (8, 4096), (8, 4096), shape((TD, PAIRS), BF16)],
        sources,
        [parts, pltpu.SemaphoreType.DMA((5,))],
        HBM,
    )
    grad0 = reduced(local)
    local, picks, shift = call(
        first_forward,
        "fwd0",
        [(coefs * IMAGE, 128), shape((2 * PAIRS, 128), BF16), shape((PAIRS, 128), I32)],
        [geom, frac, knot, patt, grad0],
        [chosen],
    )
    got = exchange(local, "coef", coefs)
    local, image0, gamma0 = call(
        later_back, "back1", [(TABLE, 128), (32, 128), (8, 128)], [geom, place, high, types, got], [parts]
    )
    other = reduced(local)
    local, grad1 = call(
        later_forward,
        "fwd1",
        [(coefs * IMAGE, 128), (TABLE, 128)],
        [geom, frac, knot, picks, shift, grad0, other, gamma0],
        [chosen],
    )
    got = exchange(local, "coef", coefs)
    local, image1, gamma1 = call(
        norm_kernel, "norm", [(frames * doms, 128), (32, 128), (8, 128)], [got, gamma0, image0]
    )
    got = exchange(local, ("frame", "dom"), frames * doms)
    sol, resid = call(
        last_kernel,
        "last",
        [(NK, TD), (32, 128)],
        [got, gamma0, gamma1, grad0, other, grad1, image0, image1, target],
    )
    return sol.T, resid.reshape(4096)


def solution(mesh):
    in_specs = (
        P("coef", ("frame", "dom")),
        P("coef", ("frame", "dom")),
        P("coef", ("frame", "dom")),
        P("coef", ("frame", "dom")),
        P(("frame", "dom")),
    )
    out_specs = (P("coef", None), P(("frame", "dom")))
    return jax.shard_map(on_device, mesh=mesh, in_specs=in_specs, out_specs=out_specs, check_vma=False)
```

```python
import functools

import jax
import jax.numpy as jnp
from jax import lax
from jax.experimental import pallas as pl
from jax.experimental.pallas import tpu as pltpu
from jax.sharding import PartitionSpec as P

NK = 160
TYPES = 384
TD = 96
HIGH = 24
KNOTS = TD + HIGH
TABLE = 128
PAIRS = 256
IMAGE = 40
UNROLL = 8
TILES_DEV = 32

VMEM = pl.BlockSpec(memory_space=pltpu.VMEM)
HBM = pl.BlockSpec(memory_space=pltpu.HBM)
F32 = jnp.float32
BF16 = jnp.bfloat16
I32 = jnp.int32


def call(kernel, name, outs, args, scratch=(), space=VMEM):
    outs = [o if isinstance(o, jax.ShapeDtypeStruct) else jax.ShapeDtypeStruct(o, F32) for o in outs]
    return pl.pallas_call(
        kernel,
        out_shape=outs,
        in_specs=[space] * len(args),
        out_specs=[VMEM] * len(outs),
        scratch_shapes=list(scratch),
        name=name,
        compiler_params=pltpu.CompilerParams(vmem_limit_bytes=8 << 20),
    )(*args)


def split(value):
    high = value.astype(BF16)
    return high, (value - high.astype(F32)).astype(BF16)


def total_of(value):
    return jnp.sum(jnp.sum(value, axis=0, keepdims=True), axis=1, keepdims=True)


def parts_sum(ref, count, rows):
    total = ref[0:rows, :]
    for at in range(1, count):
        total = total + ref[at * rows : (at + 1) * rows, :]
    return total


def weights(u):
    square = u * u
    cube = square * u
    rest = 1.0 - u
    return (
        rest * rest * rest * (1.0 / 6.0),
        (3.0 * cube - 6.0 * square + 4.0) * (1.0 / 6.0),
        (-3.0 * cube + 3.0 * square + 3.0 * u + 1.0) * (1.0 / 6.0),
        cube * (1.0 / 6.0),
    )


def prepare(frac_ref, knot_ref, patt_ref, place_ref, high_ref, picks_ref):
    knot = knot_ref[...]
    high = (knot * 205) >> 10
    place_ref[...] = (knot - 5 * high + 1).astype(F32) + frac_ref[...]
    high_ref[...] = high.astype(F32)
    lane = lax.broadcasted_iota(I32, (8, 128), 1)
    picks = [jnp.where(lane == patt_ref[:, t : t + 1], 1.0, 0.0) for t in range(TILES_DEV)]
    picks_ref[...] = jnp.transpose(jnp.concatenate(picks, axis=0))[0:TD, :].astype(BF16)


def transposed(geom_ref, place_ref, high_ref, picks_ref, resid_ref, total, out_ref, parts_ref):
    places = lax.broadcasted_iota(I32, (8, 128), 0).astype(F32)
    rows = lax.broadcasted_iota(I32, (2, 16, 128), 0) * 16 + lax.broadcasted_iota(I32, (2, 16, 128), 1)
    rows = rows.astype(F32).astype(BF16)
    one, zero = jnp.ones((), BF16), jnp.zeros((), BF16)
    empty = jnp.zeros((16, 128), BF16)

    def tile(t):
        lanes = pl.ds(pl.multiple_of(t * 128, 128), 128)
        resid = jnp.broadcast_to(resid_ref[pl.ds(t, 1), :], (8, 128)) * (1.0 / 6.0)
        for pair in range(4):
            values, hits = [], []
            for half in range(2):
                s = slice(2 * pair + half, 2 * pair + half + 1)
                near = jnp.abs(jnp.broadcast_to(place_ref[s, lanes], (8, 128)) - places)
                a = jnp.maximum(2.0 - near, 0.0)
                b = jnp.maximum(1.0 - near, 0.0)
                amount = jnp.broadcast_to(geom_ref[s, lanes], (8, 128)) * resid
                value = amount * (a * a * a - (4.0 * b) * (b * b))
                rounded = value.astype(BF16).astype(F32)
                values.append(jnp.concatenate([rounded, value - rounded], axis=0).astype(BF16))
                at = jnp.broadcast_to(high_ref[s, lanes], (16, 128)).astype(BF16)
                hits.append(jnp.where(rows == at[None], one, zero).reshape(32, 128))
            left = jnp.concatenate(
                [jnp.concatenate([values[0], empty], axis=1), jnp.concatenate([empty, values[1]], axis=1)], axis=0
            )
            got = lax.dot_general(
                left, jnp.concatenate(hits, axis=1), (((1,), (1,)), ((), ())), preferred_element_type=F32
            )
            at = pl.ds(pl.multiple_of((t * 4 + pair) * 16, 16), 16)
            parts_ref[at, 0:32] = jnp.concatenate([got[0:8] + got[8:16], got[16:24] + got[24:32]], axis=0)

    def tiles(step, _):
        for at in range(UNROLL):
            tile(step * UNROLL + at)
        return 0

    lax.fori_loop(0, TILES_DEV // UNROLL, tiles, 0)

    picks = picks_ref[...]
    block = lax.broadcasted_iota(I32, (PAIRS, 128), 1) >> 5
    halves = []
    for group in range(2):
        piece = parts_ref[pl.ds(4 * group, PAIRS, stride=8), :]
        for q in range(1, 4):
            other = pltpu.roll(parts_ref[pl.ds(4 * group + q, PAIRS, stride=8), :], 32 * q, 1)
            piece = jnp.where(block >= q, other, piece)
        halves.append(piece)
    high, low = split(jnp.concatenate(halves, axis=1))
    grad = jnp.dot(picks, high, preferred_element_type=F32) + jnp.dot(picks, low, preferred_element_type=F32)
    source = lax.broadcasted_iota(I32, (256, 256), 0)
    column = lax.broadcasted_iota(I32, (256, 256), 1)
    knot = jnp.where(column >= 128, 128 + (column & 31), column)
    spread = jnp.where(5 * (source & 31) + (source >> 5) == knot, 1.0, 0.0).astype(BF16)
    high, low = split(grad)
    grad = jnp.dot(high, spread, preferred_element_type=F32) + jnp.dot(low, spread, preferred_element_type=F32)
    out_ref[0:TD, :] = grad[:, 0:128]
    packed = grad[0:HIGH, 128:256]
    for q in range(1, 4):
        packed = jnp.where(block[0:HIGH] >= q, grad[q * HIGH : (q + 1) * HIGH, 128:256], packed)
    out_ref[TD:KNOTS, :] = packed
    sub = lax.broadcasted_iota(I32, (8, 128), 0)
    out_ref[KNOTS:TABLE, :] = jnp.where(sub == 0, total, 0.0)


def choose(patt_ref, picks_ref, shift_ref):
    lane = lax.broadcasted_iota(I32, (8, 128), 1)
    low_rows, high_rows = [], []
    for t in range(TILES_DEV):
        kind = jnp.broadcast_to(patt_ref[:, t : t + 1], (8, 128))
        block = jnp.where(kind >= HIGH, 1, 0) + jnp.where(kind >= 2 * HIGH, 1, 0) + jnp.where(kind >= 3 * HIGH, 1, 0)
        low_rows.append(jnp.where(lane == kind, 1.0, 0.0))
        high_rows.append(jnp.where(lane == TD + kind - HIGH * block, 1.0, 0.0))
        shift_ref[8 * t : 8 * t + 8, :] = 32 * block
    picks_ref[...] = jnp.concatenate(low_rows + high_rows, axis=0).astype(BF16)


def applied(geom_ref, frac_ref, knot_ref, picks_ref, shift_ref, table, out_ref, chosen_ref):
    picks = picks_ref[...]
    high, low = split(table)
    chosen_ref[...] = jnp.dot(picks, high, preferred_element_type=F32) + jnp.dot(
        picks, low, preferred_element_type=F32
    )
    for t in range(TILES_DEV):
        lanes = slice(128 * t, 128 * (t + 1))
        slots = slice(8 * t, 8 * t + 8)
        base = knot_ref[:, lanes]
        first = chosen_ref[slots, :]
        last = chosen_ref[PAIRS + 8 * t : PAIRS + 8 * t + 8, :]
        value = None
        for j, weight in enumerate(weights(frac_ref[:, lanes])):
            at = base + j
            near = jnp.take_along_axis(first, at & 127, axis=1, mode="promise_in_bounds")
            far = jnp.take_along_axis(last, (at & 31) + shift_ref[slots, :], axis=1, mode="promise_in_bounds")
            term = weight * jnp.where(at >= 128, far, near)
            value = term if j == 0 else value + term
        row = jnp.sum(geom_ref[:, lanes] * value, axis=0, keepdims=True)
        for c in range(out_ref.shape[0] // IMAGE):
            out_ref[c * IMAGE + t : c * IMAGE + t + 1, :] = row
    gamma = jnp.broadcast_to(total_of(table[0:KNOTS] * table[0:KNOTS]), (8, 128))
    for c in range(out_ref.shape[0] // IMAGE):
        out_ref[c * IMAGE + 32 : (c + 1) * IMAGE, :] = gamma


def first_back(*refs):
    sources, (out, *copies), (place, high, picks), (parts, sems) = refs[:5], refs[5:11], refs[11:14], refs[14:]
    moves = [pltpu.make_async_copy(a, b, sems.at[i]) for i, (a, b) in enumerate(zip(sources, copies, strict=True))]
    for move in moves:
        move.start()
    for move in moves:
        move.wait()
    geom, frac, knot, patt, target = copies
    prepare(frac, knot, patt, place, high, picks)
    transposed(geom, place, high, picks, target, 0.0, out, parts)


def later_back(geom, place, high, picks, got, out, image, gamma, parts):
    whole = parts_sum(got, got.shape[0] // IMAGE, IMAGE)
    image[...] = whole[0:32]
    gamma[...] = whole[32:40]
    total = jnp.broadcast_to(total_of(whole[0:32] * whole[0:32]), (8, 128))
    transposed(geom, place, high, picks, image, total, out, parts)


def scattered(count, copies, got, out):
    rows = got.shape[0] // count
    total = parts_sum(got, count, rows)
    for at in range(copies):
        out[at * rows : (at + 1) * rows, :] = total


def first_forward(geom, frac, knot, patt, grad, out, picks, shift, chosen):
    choose(patt, picks, shift)
    applied(geom, frac, knot, picks, shift, grad[...], out, chosen)


def later_forward(geom, frac, knot, picks, shift, grad, other, gamma, out, table, chosen):
    alpha = gamma[0:1, :] / other[KNOTS : KNOTS + 1, :]
    table[...] = grad[...] - alpha * other[...]
    applied(geom, frac, knot, picks, shift, table[...], out, chosen)


def norm_kernel(got, gamma, image, out, image_out, gamma_out):
    whole = parts_sum(got, got.shape[0] // IMAGE, IMAGE)
    gamma_out[...] = whole[32:40]
    beta = whole[32:33] / gamma[0:1, :]
    result = whole[0:32] + beta * image[...]
    image_out[...] = result
    out[...] = jnp.broadcast_to(total_of(result * result), out.shape)


def last_kernel(got, gamma0, gamma1, grad0, other, grad1, image0, image1, target, sol, resid):
    total1 = jnp.sum(got[...], axis=0, keepdims=True)
    alpha0 = gamma0[0:1, :] / other[KNOTS : KNOTS + 1, :]
    alpha1 = gamma1[0:1, :] / total1
    beta = gamma1[0:1, :] / gamma0[0:1, :]
    resid[...] = target[...] - alpha0 * image0[...] - alpha1 * image1[...]
    table = alpha0 * grad0[...] + alpha1 * (grad1[...] + beta * grad0[...])
    turned = jnp.transpose(table)
    sol[0:128, :] = turned[:, 0:TD]
    lane = lax.broadcasted_iota(I32, (32, 128), 1)
    top = pltpu.roll(turned[0:32], 128 - TD, 1)
    for q in range(1, 4):
        piece = pltpu.roll(turned[32 * q : 32 * q + 32], (128 - TD + HIGH * q) % 128, 1)
        top = jnp.where(lane >= HIGH * q, piece, top)
    sol[128:NK, :] = top[:, 0:TD]


def exchange(value, axis, count):
    rows = value.shape[0]
    got = lax.all_to_all(value.reshape(count, rows * 128 // count), axis, 0, 0, tiled=True)
    return got.reshape(rows, 128)


def on_device(geometry, fraction, interval, pattern, target):
    frames, doms, coefs = lax.axis_size("frame"), lax.axis_size("dom"), lax.axis_size("coef")
    piece = TABLE // doms
    shape = jax.ShapeDtypeStruct
    parts = pltpu.VMEM((8 * PAIRS, 128), F32)
    chosen = pltpu.VMEM((2 * PAIRS, 128), F32)

    def reduced(local):
        got = exchange(local, "dom", doms)
        (mine,) = call(functools.partial(scattered, doms, frames), "scatter_dom", [(frames * piece, 128)], [got])
        got = exchange(mine, "frame", frames)
        (mine,) = call(functools.partial(scattered, frames, doms), "scatter_frame", [(TABLE, 128)], [got])
        return exchange(mine, "dom", doms)

    sources = [geometry, fraction, interval, pattern, target.reshape(32, 128)]
    copies = [shape(s.shape, s.dtype) for s in sources]
    sources = [pltpu.with_memory_space_constraint(s, pltpu.HBM) for s in sources]
    local, geom, frac, knot, patt, target, place, high, types = call(
        first_back,
        "back0",
        [(TABLE, 128), *copies, (8, 4096), (8, 4096), shape((TD, PAIRS), BF16)],
        sources,
        [parts, pltpu.SemaphoreType.DMA((5,))],
        HBM,
    )
    grad0 = reduced(local)
    local, picks, shift = call(
        first_forward,
        "fwd0",
        [(coefs * IMAGE, 128), shape((2 * PAIRS, 128), BF16), shape((PAIRS, 128), I32)],
        [geom, frac, knot, patt, grad0],
        [chosen],
    )
    got = exchange(local, "coef", coefs)
    local, image0, gamma0 = call(
        later_back, "back1", [(TABLE, 128), (32, 128), (8, 128)], [geom, place, high, types, got], [parts]
    )
    other = reduced(local)
    local, grad1 = call(
        later_forward,
        "fwd1",
        [(coefs * IMAGE, 128), (TABLE, 128)],
        [geom, frac, knot, picks, shift, grad0, other, gamma0],
        [chosen],
    )
    got = exchange(local, "coef", coefs)
    local, image1, gamma1 = call(
        norm_kernel, "norm", [(frames * doms, 128), (32, 128), (8, 128)], [got, gamma0, image0]
    )
    got = exchange(local, ("frame", "dom"), frames * doms)
    sol, resid = call(
        last_kernel,
        "last",
        [(NK, TD), (32, 128)],
        [got, gamma0, gamma1, grad0, other, grad1, image0, image1, target],
    )
    return sol.T, resid.reshape(4096)


def solution(mesh):
    in_specs = (
        P("coef", ("frame", "dom")),
        P("coef", ("frame", "dom")),
        P("coef", ("frame", "dom")),
        P("coef", ("frame", "dom")),
        P(("frame", "dom")),
    )
    out_specs = (P("coef", None), P(("frame", "dom")))
    return jax.shard_map(on_device, mesh=mesh, in_specs=in_specs, out_specs=out_specs, check_vma=False)
```

```python
import functools

import jax
import jax.numpy as jnp
from jax import lax
from jax.experimental import pallas as pl
from jax.experimental.pallas import tpu as pltpu
from jax.sharding import PartitionSpec as P

NK = 160
TYPES = 384
TD = 96
HIGH = 24
KNOTS = TD + HIGH
TABLE = 128
PAIRS = 256
IMAGE = 40
UNROLL = 8
TILES_DEV = 32

VMEM = pl.BlockSpec(memory_space=pltpu.VMEM)
HBM = pl.BlockSpec(memory_space=pltpu.HBM)
F32 = jnp.float32
BF16 = jnp.bfloat16
I32 = jnp.int32


def call(kernel, name, outs, args, scratch=(), space=VMEM):
    outs = [o if isinstance(o, jax.ShapeDtypeStruct) else jax.ShapeDtypeStruct(o, F32) for o in outs]
    return pl.pallas_call(
        kernel,
        out_shape=outs,
        in_specs=[space] * len(args),
        out_specs=[VMEM] * len(outs),
        scratch_shapes=list(scratch),
        name=name,
        compiler_params=pltpu.CompilerParams(vmem_limit_bytes=8 << 20),
    )(*args)


def split(value):
    high = value.astype(BF16)
    return high, (value - high.astype(F32)).astype(BF16)


def total_of(value):
    return jnp.sum(jnp.sum(value, axis=0, keepdims=True), axis=1, keepdims=True)


def parts_sum(ref, count, rows):
    total = ref[0:rows, :]
    for at in range(1, count):
        total = total + ref[at * rows : (at + 1) * rows, :]
    return total


def weights(u):
    square = u * u
    cube = square * u
    rest = 1.0 - u
    return (
        rest * rest * rest * (1.0 / 6.0),
        (3.0 * cube - 6.0 * square + 4.0) * (1.0 / 6.0),
        (-3.0 * cube + 3.0 * square + 3.0 * u + 1.0) * (1.0 / 6.0),
        cube * (1.0 / 6.0),
    )


def prepare(frac_ref, knot_ref, patt_ref, place_ref, high_ref, picks_ref):
    knot = knot_ref[...]
    high = (knot * 205) >> 10
    place_ref[...] = (knot - 5 * high + 1).astype(F32) + frac_ref[...]
    high_ref[...] = high.astype(F32)
    lane = lax.broadcasted_iota(I32, (8, 128), 1)
    picks = [jnp.where(lane == patt_ref[:, t : t + 1], 1.0, 0.0) for t in range(TILES_DEV)]
    picks_ref[...] = jnp.transpose(jnp.concatenate(picks, axis=0))[0:TD, :].astype(BF16)


def transposed(geom_ref, place_ref, high_ref, picks_ref, resid_ref, total, out_ref, parts_ref):
    places = lax.broadcasted_iota(I32, (8, 128), 0).astype(F32)
    rows = lax.broadcasted_iota(I32, (2, 16, 128), 0) * 16 + lax.broadcasted_iota(I32, (2, 16, 128), 1)
    rows = rows.astype(F32).astype(BF16)
    one, zero = jnp.ones((), BF16), jnp.zeros((), BF16)
    empty = jnp.zeros((16, 128), BF16)

    def tile(t):
        lanes = pl.ds(pl.multiple_of(t * 128, 128), 128)
        resid = jnp.broadcast_to(resid_ref[pl.ds(t, 1), :], (8, 128)) * (1.0 / 6.0)
        for pair in range(4):
            values, hits = [], []
            for half in range(2):
                s = slice(2 * pair + half, 2 * pair + half + 1)
                near = jnp.abs(jnp.broadcast_to(place_ref[s, lanes], (8, 128)) - places)
                a = jnp.maximum(2.0 - near, 0.0)
                b = jnp.maximum(1.0 - near, 0.0)
                amount = jnp.broadcast_to(geom_ref[s, lanes], (8, 128)) * resid
                value = amount * (a * a * a - (4.0 * b) * (b * b))
                rounded = value.astype(BF16).astype(F32)
                values.append(jnp.concatenate([rounded, value - rounded], axis=0).astype(BF16))
                at = jnp.broadcast_to(high_ref[s, lanes], (16, 128)).astype(BF16)
                hits.append(jnp.where(rows == at[None], one, zero).reshape(32, 128))
            left = jnp.concatenate(
                [jnp.concatenate([values[0], empty], axis=1), jnp.concatenate([empty, values[1]], axis=1)], axis=0
            )
            got = lax.dot_general(
                left, jnp.concatenate(hits, axis=1), (((1,), (1,)), ((), ())), preferred_element_type=F32
            )
            at = pl.ds(pl.multiple_of((t * 4 + pair) * 16, 16), 16)
            parts_ref[at, 0:32] = jnp.concatenate([got[0:8] + got[8:16], got[16:24] + got[24:32]], axis=0)

    def tiles(step, _):
        for at in range(UNROLL):
            tile(step * UNROLL + at)
        return 0

    lax.fori_loop(0, TILES_DEV // UNROLL, tiles, 0)

    picks = picks_ref[...]
    block = lax.broadcasted_iota(I32, (PAIRS, 128), 1) >> 5
    halves = []
    for group in range(2):
        piece = parts_ref[pl.ds(4 * group, PAIRS, stride=8), :]
        for q in range(1, 4):
            other = pltpu.roll(parts_ref[pl.ds(4 * group + q, PAIRS, stride=8), :], 32 * q, 1)
            piece = jnp.where(block >= q, other, piece)
        halves.append(piece)
    high, low = split(jnp.concatenate(halves, axis=1))
    grad = jnp.dot(picks, high, preferred_element_type=F32) + jnp.dot(picks, low, preferred_element_type=F32)
    source = lax.broadcasted_iota(I32, (256, 256), 0)
    column = lax.broadcasted_iota(I32, (256, 256), 1)
    knot = jnp.where(column >= 128, 128 + (column & 31), column)
    spread = jnp.where(5 * (source & 31) + (source >> 5) == knot, 1.0, 0.0).astype(BF16)
    high, low = split(grad)
    grad = jnp.dot(high, spread, preferred_element_type=F32) + jnp.dot(low, spread, preferred_element_type=F32)
    out_ref[0:TD, :] = grad[:, 0:128]
    packed = grad[0:HIGH, 128:256]
    for q in range(1, 4):
        packed = jnp.where(block[0:HIGH] >= q, grad[q * HIGH : (q + 1) * HIGH, 128:256], packed)
    out_ref[TD:KNOTS, :] = packed
    sub = lax.broadcasted_iota(I32, (8, 128), 0)
    out_ref[KNOTS:TABLE, :] = jnp.where(sub == 0, total, 0.0)


def choose(patt_ref, picks_ref, shift_ref):
    lane = lax.broadcasted_iota(I32, (8, 128), 1)
    low_rows, high_rows = [], []
    for t in range(TILES_DEV):
        kind = jnp.broadcast_to(patt_ref[:, t : t + 1], (8, 128))
        block = jnp.where(kind >= HIGH, 1, 0) + jnp.where(kind >= 2 * HIGH, 1, 0) + jnp.where(kind >= 3 * HIGH, 1, 0)
        low_rows.append(jnp.where(lane == kind, 1.0, 0.0))
        high_rows.append(jnp.where(lane == TD + kind - HIGH * block, 1.0, 0.0))
        shift_ref[8 * t : 8 * t + 8, :] = 32 * block
    picks_ref[...] = jnp.concatenate(low_rows + high_rows, axis=0).astype(BF16)


def applied(geom_ref, frac_ref, knot_ref, picks_ref, shift_ref, table, out_ref, chosen_ref):
    picks = picks_ref[...]
    high, low = split(table)
    chosen_ref[...] = jnp.dot(picks, high, preferred_element_type=F32) + jnp.dot(
        picks, low, preferred_element_type=F32
    )
    for t in range(TILES_DEV):
        lanes = slice(128 * t, 128 * (t + 1))
        slots = slice(8 * t, 8 * t + 8)
        base = knot_ref[:, lanes]
        first = chosen_ref[slots, :]
        last = chosen_ref[PAIRS + 8 * t : PAIRS + 8 * t + 8, :]
        value = None
        for j, weight in enumerate(weights(frac_ref[:, lanes])):
            at = base + j
            near = jnp.take_along_axis(first, at & 127, axis=1, mode="promise_in_bounds")
            far = jnp.take_along_axis(last, (at & 31) + shift_ref[slots, :], axis=1, mode="promise_in_bounds")
            term = weight * jnp.where(at >= 128, far, near)
            value = term if j == 0 else value + term
        row = jnp.sum(geom_ref[:, lanes] * value, axis=0, keepdims=True)
        for c in range(out_ref.shape[0] // IMAGE):
            out_ref[c * IMAGE + t : c * IMAGE + t + 1, :] = row
    gamma = jnp.broadcast_to(total_of(table[0:KNOTS] * table[0:KNOTS]), (8, 128))
    for c in range(out_ref.shape[0] // IMAGE):
        out_ref[c * IMAGE + 32 : (c + 1) * IMAGE, :] = gamma


def first_back(*refs):
    sources, (out, *copies), (place, high, picks), (parts, sems) = refs[:5], refs[5:11], refs[11:14], refs[14:]
    moves = [pltpu.make_async_copy(a, b, sems.at[i]) for i, (a, b) in enumerate(zip(sources, copies, strict=True))]
    for move in moves:
        move.start()
    for move in moves:
        move.wait()
    geom, frac, knot, patt, target = copies
    prepare(frac, knot, patt, place, high, picks)
    transposed(geom, place, high, picks, target, 0.0, out, parts)


def later_back(geom, place, high, picks, got, out, image, gamma, parts):
    whole = parts_sum(got, got.shape[0] // IMAGE, IMAGE)
    image[...] = whole[0:32]
    gamma[...] = whole[32:40]
    total = jnp.broadcast_to(total_of(whole[0:32] * whole[0:32]), (8, 128))
    transposed(geom, place, high, picks, image, total, out, parts)


def scattered(count, groups, copies, got, out):
    rows = got.shape[0] // count
    for group in range(groups):
        total = got[group * rows : (group + 1) * rows, :]
        for at in range(group + groups, count, groups):
            total = total + got[at * rows : (at + 1) * rows, :]
        for at in range(copies):
            out[(at * groups + group) * rows : (at * groups + group + 1) * rows, :] = total


def first_forward(geom, frac, knot, patt, grad, out, picks, shift, chosen):
    choose(patt, picks, shift)
    applied(geom, frac, knot, picks, shift, grad[...], out, chosen)


def later_forward(geom, frac, knot, picks, shift, grad, other, gamma, out, table, chosen):
    alpha = gamma[0:1, :] / other[KNOTS : KNOTS + 1, :]
    table[...] = grad[...] - alpha * other[...]
    applied(geom, frac, knot, picks, shift, table[...], out, chosen)


def norm_kernel(got, gamma, image, out, image_out, gamma_out):
    whole = parts_sum(got, got.shape[0] // IMAGE, IMAGE)
    gamma_out[...] = whole[32:40]
    beta = whole[32:33] / gamma[0:1, :]
    result = whole[0:32] + beta * image[...]
    image_out[...] = result
    out[...] = jnp.broadcast_to(total_of(result * result), out.shape)


def last_kernel(got, gamma0, gamma1, grad0, other, grad1, image0, image1, target, sol, resid):
    total1 = jnp.sum(got[...], axis=0, keepdims=True)
    alpha0 = gamma0[0:1, :] / other[KNOTS : KNOTS + 1, :]
    alpha1 = gamma1[0:1, :] / total1
    beta = gamma1[0:1, :] / gamma0[0:1, :]
    resid[...] = target[...] - alpha0 * image0[...] - alpha1 * image1[...]
    table = alpha0 * grad0[...] + alpha1 * (grad1[...] + beta * grad0[...])
    turned = jnp.transpose(table)
    sol[0:128, :] = turned[:, 0:TD]
    lane = lax.broadcasted_iota(I32, (32, 128), 1)
    top = pltpu.roll(turned[0:32], 128 - TD, 1)
    for q in range(1, 4):
        piece = pltpu.roll(turned[32 * q : 32 * q + 32], (128 - TD + HIGH * q) % 128, 1)
        top = jnp.where(lane >= HIGH * q, piece, top)
    sol[128:NK, :] = top[:, 0:TD]


def exchange(value, axis, count):
    rows = value.shape[0]
    got = lax.all_to_all(value.reshape(count, rows * 128 // count), axis, 0, 0, tiled=True)
    return got.reshape(rows, 128)


def on_device(geometry, fraction, interval, pattern, target):
    near = lax.axis_size("near")
    frames, doms, coefs = lax.axis_size("far") * near, lax.axis_size("dom"), lax.axis_size("coef")
    shape = jax.ShapeDtypeStruct
    parts = pltpu.VMEM((8 * PAIRS, 128), F32)
    chosen = pltpu.VMEM((2 * PAIRS, 128), F32)

    def reduced(local):
        got = exchange(local, ("dom", "near"), doms * near)
        mine = frames * TABLE // (doms * near)
        (mine,) = call(functools.partial(scattered, doms * near, 1, frames), "scatter_dom", [(mine, 128)], [got])
        got = exchange(mine, ("far", "near"), frames)
        (mine,) = call(functools.partial(scattered, frames, near, doms), "scatter_frame", [(TABLE, 128)], [got])
        return exchange(mine, "dom", doms)

    sources = [geometry, fraction, interval, pattern, target.reshape(32, 128)]
    copies = [shape(s.shape, s.dtype) for s in sources]
    sources = [pltpu.with_memory_space_constraint(s, pltpu.HBM) for s in sources]
    local, geom, frac, knot, patt, target, place, high, types = call(
        first_back,
        "back0",
        [(TABLE, 128), *copies, (8, 4096), (8, 4096), shape((TD, PAIRS), BF16)],
        sources,
        [parts, pltpu.SemaphoreType.DMA((5,))],
        HBM,
    )
    grad0 = reduced(local)
    local, picks, shift = call(
        first_forward,
        "fwd0",
        [(coefs * IMAGE, 128), shape((2 * PAIRS, 128), BF16), shape((PAIRS, 128), I32)],
        [geom, frac, knot, patt, grad0],
        [chosen],
    )
    got = exchange(local, "coef", coefs)
    local, image0, gamma0 = call(
        later_back, "back1", [(TABLE, 128), (32, 128), (8, 128)], [geom, place, high, types, got], [parts]
    )
    other = reduced(local)
    local, grad1 = call(
        later_forward,
        "fwd1",
        [(coefs * IMAGE, 128), (TABLE, 128)],
        [geom, frac, knot, picks, shift, grad0, other, gamma0],
        [chosen],
    )
    got = exchange(local, "coef", coefs)
    local, image1, gamma1 = call(
        norm_kernel, "norm", [(frames * doms, 128), (32, 128), (8, 128)], [got, gamma0, image0]
    )
    got = exchange(local, ("far", "near", "dom"), frames * doms)
    sol, resid = call(
        last_kernel,
        "last",
        [(NK, TD), (32, 128)],
        [got, gamma0, gamma1, grad0, other, grad1, image0, image1, target],
    )
    return sol.T, resid.reshape(4096)


def solution(mesh):
    frames, doms, coefs = mesh.devices.shape
    near = 2 if frames % 2 == 0 else 1
    mesh = jax.sharding.Mesh(mesh.devices.reshape(frames // near, near, doms, coefs), ("far", "near", "dom", "coef"))
    rows = ("far", "near", "dom")
    in_specs = (P("coef", rows), P("coef", rows), P("coef", rows), P("coef", rows), P(rows))
    out_specs = (P("coef", None), P(rows))
    return jax.shard_map(on_device, mesh=mesh, in_specs=in_specs, out_specs=out_specs, check_vma=False)
```

```python
import functools

import jax
import jax.numpy as jnp
from jax import lax
from jax.experimental import pallas as pl
from jax.experimental.pallas import tpu as pltpu
from jax.sharding import PartitionSpec as P

NK = 160
TYPES = 384
TD = 96
HIGH = 24
KNOTS = TD + HIGH
TABLE = 128
PAIRS = 256
IMAGE = 40
UNROLL = 16
GROUP = 8
TILES_DEV = 32

VMEM = pl.BlockSpec(memory_space=pltpu.VMEM)
HBM = pl.BlockSpec(memory_space=pltpu.HBM)
F32 = jnp.float32
BF16 = jnp.bfloat16
I32 = jnp.int32


def call(kernel, name, outs, args, scratch=(), space=VMEM):
    outs = [o if isinstance(o, jax.ShapeDtypeStruct) else jax.ShapeDtypeStruct(o, F32) for o in outs]
    return pl.pallas_call(
        kernel,
        out_shape=outs,
        in_specs=[space] * len(args),
        out_specs=[VMEM] * len(outs),
        scratch_shapes=list(scratch),
        name=name,
        compiler_params=pltpu.CompilerParams(vmem_limit_bytes=8 << 20),
    )(*args)


def split(value):
    high = value.astype(BF16)
    return high, (value - high.astype(F32)).astype(BF16)


def total_of(value):
    return jnp.sum(jnp.sum(value, axis=0, keepdims=True), axis=1, keepdims=True)


def parts_sum(ref, count, rows):
    total = ref[0:rows, :]
    for at in range(1, count):
        total = total + ref[at * rows : (at + 1) * rows, :]
    return total


def weights(u):
    square = u * u
    cube = square * u
    rest = 1.0 - u
    return (
        rest * rest * rest * (1.0 / 6.0),
        (3.0 * cube - 6.0 * square + 4.0) * (1.0 / 6.0),
        (-3.0 * cube + 3.0 * square + 3.0 * u + 1.0) * (1.0 / 6.0),
        cube * (1.0 / 6.0),
    )


def prepare(frac_ref, knot_ref, patt_ref, place_ref, high_ref, picks_ref):
    knot = knot_ref[...]
    high = (knot * 205) >> 10
    place_ref[...] = (knot - 5 * high + 1).astype(F32) + frac_ref[...]
    high_ref[...] = high.astype(F32)
    lane = lax.broadcasted_iota(I32, (8, 128), 1)
    picks = [jnp.where(lane == patt_ref[:, t : t + 1], 1.0, 0.0) for t in range(TILES_DEV)]
    picks_ref[...] = jnp.transpose(jnp.concatenate(picks, axis=0))[0:TD, :].astype(BF16)


def spreading(spread_ref):
    source = lax.broadcasted_iota(I32, (256, 256), 0)
    column = lax.broadcasted_iota(I32, (256, 256), 1)
    knot = jnp.where(column >= 128, 128 + (column & 31), column)
    spread_ref[...] = jnp.where(5 * (source & 31) + (source >> 5) == knot, 1.0, 0.0).astype(BF16)


def transposed(geom_ref, place_ref, high_ref, picks_ref, spread_ref, shape_ref, resid_ref, total, out_ref, parts_ref):
    places = lax.broadcasted_iota(I32, (8, 128), 0).astype(F32)
    rows = lax.broadcasted_iota(I32, (2, 16, 128), 0) * 16 + lax.broadcasted_iota(I32, (2, 16, 128), 1)
    rows = rows.astype(F32).astype(BF16)
    one, zero = jnp.ones((), BF16), jnp.zeros((), BF16)
    empty = jnp.zeros((16, 128), BF16)

    def tile(t):
        lanes = pl.ds(pl.multiple_of(t * 128, 128), 128)
        resid = jnp.broadcast_to(resid_ref[pl.ds(t, 1), :], (8, 128)) * (1.0 / 6.0)
        for pair in range(4):
            values, hits = [], []
            for half in range(2):
                s = slice(2 * pair + half, 2 * pair + half + 1)
                kept = pl.ds(pl.multiple_of((t * 8 + 2 * pair + half) * 8, 8), 8)
                if place_ref is None:
                    spline = shape_ref[kept, :]
                else:
                    near = jnp.abs(jnp.broadcast_to(place_ref[s, lanes], (8, 128)) - places)
                    a = jnp.maximum(2.0 - near, 0.0)
                    b = jnp.maximum(1.0 - near, 0.0)
                    spline = a * a * a - (4.0 * b) * (b * b)
                    shape_ref[kept, :] = spline
                value = jnp.broadcast_to(geom_ref[s, lanes], (8, 128)) * resid * spline
                rounded = value.astype(BF16).astype(F32)
                values.append(jnp.concatenate([rounded, value - rounded], axis=0).astype(BF16))
                at = jnp.broadcast_to(high_ref[s, lanes], (16, 128)).astype(BF16)
                hits.append(jnp.where(rows == at[None], one, zero).reshape(32, 128))
            left = jnp.concatenate(
                [jnp.concatenate([values[0], empty], axis=1), jnp.concatenate([empty, values[1]], axis=1)], axis=0
            )
            got = lax.dot_general(
                left, jnp.concatenate(hits, axis=1), (((1,), (1,)), ((), ())), preferred_element_type=F32
            )
            at = pl.ds(pl.multiple_of((t * 4 + pair) * 16, 16), 16)
            parts_ref[at, 0:32] = jnp.concatenate([got[0:8] + got[8:16], got[16:24] + got[24:32]], axis=0)

    def tiles(step, _):
        for at in range(UNROLL):
            tile(step * UNROLL + at)
        return 0

    lax.fori_loop(0, TILES_DEV // UNROLL, tiles, 0)

    picks = picks_ref[...]
    block = lax.broadcasted_iota(I32, (PAIRS, 128), 1) >> 5
    halves = []
    for group in range(2):
        piece = parts_ref[pl.ds(4 * group, PAIRS, stride=8), :]
        for q in range(1, 4):
            other = pltpu.roll(parts_ref[pl.ds(4 * group + q, PAIRS, stride=8), :], 32 * q, 1)
            piece = jnp.where(block >= q, other, piece)
        halves.append(piece)
    high, low = split(jnp.concatenate(halves, axis=1))
    grad = jnp.dot(picks, high, preferred_element_type=F32) + jnp.dot(picks, low, preferred_element_type=F32)
    spread = spread_ref[...]
    high, low = split(grad)
    grad = jnp.dot(high, spread, preferred_element_type=F32) + jnp.dot(low, spread, preferred_element_type=F32)
    out_ref[0:TD, :] = grad[:, 0:128]
    packed = grad[0:HIGH, 128:256]
    for q in range(1, 4):
        packed = jnp.where(block[0:HIGH] >= q, grad[q * HIGH : (q + 1) * HIGH, 128:256], packed)
    out_ref[TD:KNOTS, :] = packed
    sub = lax.broadcasted_iota(I32, (8, 128), 0)
    out_ref[KNOTS:TABLE, :] = jnp.where(sub == 0, total, 0.0)


def choose(patt_ref, picks_ref, shift_ref):
    lane = lax.broadcasted_iota(I32, (8, 128), 1)
    low_rows, high_rows = [], []
    for t in range(TILES_DEV):
        kind = jnp.broadcast_to(patt_ref[:, t : t + 1], (8, 128))
        block = jnp.where(kind >= HIGH, 1, 0) + jnp.where(kind >= 2 * HIGH, 1, 0) + jnp.where(kind >= 3 * HIGH, 1, 0)
        low_rows.append(jnp.where(lane == kind, 1.0, 0.0))
        high_rows.append(jnp.where(lane == TD + kind - HIGH * block, 1.0, 0.0))
        shift_ref[8 * t : 8 * t + 8, :] = 32 * block
    rows = []
    for t in range(0, TILES_DEV, GROUP):
        rows += low_rows[t : t + GROUP] + high_rows[t : t + GROUP]
    picks_ref[...] = jnp.concatenate(rows, axis=0).astype(BF16)


def applied(geom_ref, frac_ref, knot_ref, picks_ref, shift_ref, table, out_ref):
    both = jnp.concatenate(split(table), axis=1)
    gamma = jnp.broadcast_to(total_of(table[0:KNOTS] * table[0:KNOTS]), (8, 128))
    for c in range(out_ref.shape[0] // IMAGE):
        out_ref[c * IMAGE + 32 : (c + 1) * IMAGE, :] = gamma
    for t in range(TILES_DEV):
        if t % GROUP == 0:
            got = jnp.dot(picks_ref[16 * t : 16 * (t + GROUP), :], both, preferred_element_type=F32)
            chosen = got[:, 0:128] + got[:, 128:256]
        lanes = slice(128 * t, 128 * (t + 1))
        slots = slice(8 * t, 8 * t + 8)
        at = 8 * (t % GROUP)
        first = chosen[at : at + 8]
        last = chosen[8 * GROUP + at : 8 * GROUP + at + 8]
        base = knot_ref[:, lanes]
        value = None
        for j, weight in enumerate(weights(frac_ref[:, lanes])):
            at = base + j
            near = jnp.take_along_axis(first, at & 127, axis=1, mode="promise_in_bounds")
            far = jnp.take_along_axis(last, (at & 31) + shift_ref[slots, :], axis=1, mode="promise_in_bounds")
            term = weight * jnp.where(at >= 128, far, near)
            value = term if j == 0 else value + term
        row = jnp.sum(geom_ref[:, lanes] * value, axis=0, keepdims=True)
        for c in range(out_ref.shape[0] // IMAGE):
            out_ref[c * IMAGE + t : c * IMAGE + t + 1, :] = row


def first_back(*refs):
    sources, (out, *copies), (high, picks, spread, splines) = refs[:5], refs[5:11], refs[11:15]
    place, parts, sems = refs[15:]
    moves = [pltpu.make_async_copy(a, b, sems.at[i]) for i, (a, b) in enumerate(zip(sources, copies, strict=True))]
    for move in moves:
        move.start()
    spreading(spread)
    for move in moves:
        move.wait()
    geom, frac, knot, patt, target = copies
    prepare(frac, knot, patt, place, high, picks)
    transposed(geom, place, high, picks, spread, splines, target, 0.0, out, parts)


def later_back(geom, high, picks, spread, splines, got, out, image, gamma, parts):
    whole = parts_sum(got, got.shape[0] // IMAGE, IMAGE)
    image[...] = whole[0:32]
    gamma[...] = whole[32:40]
    total = jnp.broadcast_to(total_of(whole[0:32] * whole[0:32]), (8, 128))
    transposed(geom, None, high, picks, spread, splines, image, total, out, parts)


def scattered(count, groups, copies, got, out):
    rows = got.shape[0] // count
    for group in range(groups):
        total = got[group * rows : (group + 1) * rows, :]
        for at in range(group + groups, count, groups):
            total = total + got[at * rows : (at + 1) * rows, :]
        for at in range(copies):
            out[(at * groups + group) * rows : (at * groups + group + 1) * rows, :] = total


def first_forward(geom, frac, knot, patt, grad, out, picks, shift):
    choose(patt, picks, shift)
    applied(geom, frac, knot, picks, shift, grad[...], out)


def later_forward(geom, frac, knot, picks, shift, grad, other, gamma, out, table):
    alpha = gamma[0:1, :] / other[KNOTS : KNOTS + 1, :]
    table[...] = grad[...] - alpha * other[...]
    applied(geom, frac, knot, picks, shift, table[...], out)


def norm_kernel(got, gamma, image, out, image_out, gamma_out):
    whole = parts_sum(got, got.shape[0] // IMAGE, IMAGE)
    gamma_out[...] = whole[32:40]
    beta = whole[32:33] / gamma[0:1, :]
    result = whole[0:32] + beta * image[...]
    image_out[...] = result
    out[...] = jnp.broadcast_to(total_of(result * result), out.shape)


def last_kernel(got, gamma0, gamma1, grad0, other, grad1, image0, image1, target, sol, resid):
    total1 = jnp.sum(got[...], axis=0, keepdims=True)
    alpha0 = gamma0[0:1, :] / other[KNOTS : KNOTS + 1, :]
    alpha1 = gamma1[0:1, :] / total1
    beta = gamma1[0:1, :] / gamma0[0:1, :]
    resid[...] = target[...] - alpha0 * image0[...] - alpha1 * image1[...]
    table = alpha0 * grad0[...] + alpha1 * (grad1[...] + beta * grad0[...])
    turned = jnp.transpose(table)
    sol[0:128, :] = turned[:, 0:TD]
    lane = lax.broadcasted_iota(I32, (32, 128), 1)
    top = pltpu.roll(turned[0:32], 128 - TD, 1)
    for q in range(1, 4):
        piece = pltpu.roll(turned[32 * q : 32 * q + 32], (128 - TD + HIGH * q) % 128, 1)
        top = jnp.where(lane >= HIGH * q, piece, top)
    sol[128:NK, :] = top[:, 0:TD]


def exchange(value, axis, count):
    rows = value.shape[0]
    got = lax.all_to_all(value.reshape(count, rows * 128 // count), axis, 0, 0, tiled=True)
    return got.reshape(rows, 128)


def on_device(geometry, fraction, interval, pattern, target):
    near = lax.axis_size("near")
    frames, doms, coefs = lax.axis_size("far") * near, lax.axis_size("dom"), lax.axis_size("coef")
    shape = jax.ShapeDtypeStruct
    parts = pltpu.VMEM((8 * PAIRS, 128), F32)

    def reduced(local):
        got = exchange(local, ("dom", "near"), doms * near)
        mine = frames * TABLE // (doms * near)
        (mine,) = call(functools.partial(scattered, doms * near, 1, frames), "scatter_dom", [(mine, 128)], [got])
        got = exchange(mine, ("far", "near"), frames)
        (mine,) = call(functools.partial(scattered, frames, near, doms), "scatter_frame", [(TABLE, 128)], [got])
        return exchange(mine, "dom", doms)

    sources = [geometry, fraction, interval, pattern, target.reshape(32, 128)]
    copies = [shape(s.shape, s.dtype) for s in sources]
    sources = [pltpu.with_memory_space_constraint(s, pltpu.HBM) for s in sources]
    local, geom, frac, knot, patt, target, high, types, spread, splines = call(
        first_back,
        "back0",
        [(TABLE, 128), *copies, (8, 4096), shape((TD, PAIRS), BF16), shape((256, 256), BF16), (8 * PAIRS, 128)],
        sources,
        [pltpu.VMEM((8, 4096), F32), parts, pltpu.SemaphoreType.DMA((5,))],
        HBM,
    )
    grad0 = reduced(local)
    local, picks, shift = call(
        first_forward,
        "fwd0",
        [(coefs * IMAGE, 128), shape((2 * PAIRS, 128), BF16), shape((PAIRS, 128), I32)],
        [geom, frac, knot, patt, grad0],
    )
    got = exchange(local, "coef", coefs)
    local, image0, gamma0 = call(
        later_back, "back1", [(TABLE, 128), (32, 128), (8, 128)], [geom, high, types, spread, splines, got], [parts]
    )
    other = reduced(local)
    local, grad1 = call(
        later_forward,
        "fwd1",
        [(coefs * IMAGE, 128), (TABLE, 128)],
        [geom, frac, knot, picks, shift, grad0, other, gamma0],
    )
    got = exchange(local, "coef", coefs)
    local, image1, gamma1 = call(
        norm_kernel, "norm", [(frames * doms, 128), (32, 128), (8, 128)], [got, gamma0, image0]
    )
    got = exchange(local, ("far", "near", "dom"), frames * doms)
    sol, resid = call(
        last_kernel,
        "last",
        [(NK, TD), (32, 128)],
        [got, gamma0, gamma1, grad0, other, grad1, image0, image1, target],
    )
    return sol.T, resid.reshape(4096)


def solution(mesh):
    frames, doms, coefs = mesh.devices.shape
    near = 2 if frames % 2 == 0 else 1
    mesh = jax.sharding.Mesh(mesh.devices.reshape(frames // near, near, doms, coefs), ("far", "near", "dom", "coef"))
    rows = ("far", "near", "dom")
    in_specs = (P("coef", rows), P("coef", rows), P("coef", rows), P("coef", rows), P(rows))
    out_specs = (P("coef", None), P(rows))
    return jax.shard_map(on_device, mesh=mesh, in_specs=in_specs, out_specs=out_specs, check_vma=False)
```

```python
import functools

import jax
import jax.numpy as jnp
from jax import lax
from jax.experimental import pallas as pl
from jax.experimental.pallas import tpu as pltpu
from jax.sharding import PartitionSpec as P

NK = 160
TYPES = 384
TD = 96
HIGH = 24
KNOTS = TD + HIGH
TABLE = 128
PAIRS = 256
IMAGE = 40
UNROLL = 16
GROUP = 8
TILES_DEV = 32

VMEM = pl.BlockSpec(memory_space=pltpu.VMEM)
HBM = pl.BlockSpec(memory_space=pltpu.HBM)
F32 = jnp.float32
BF16 = jnp.bfloat16
I32 = jnp.int32


def call(kernel, name, outs, args, scratch=(), space=VMEM):
    outs = [o if isinstance(o, jax.ShapeDtypeStruct) else jax.ShapeDtypeStruct(o, F32) for o in outs]
    return pl.pallas_call(
        kernel,
        out_shape=outs,
        in_specs=[space] * len(args),
        out_specs=[VMEM] * len(outs),
        scratch_shapes=list(scratch),
        name=name,
        compiler_params=pltpu.CompilerParams(vmem_limit_bytes=8 << 20),
    )(*args)


def split(value):
    high = value.astype(BF16)
    return high, (value - high.astype(F32)).astype(BF16)


def total_of(value):
    return jnp.sum(jnp.sum(value, axis=0, keepdims=True), axis=1, keepdims=True)


def parts_sum(ref, count, rows):
    total = ref[0:rows, :]
    for at in range(1, count):
        total = total + ref[at * rows : (at + 1) * rows, :]
    return total


def weights(u):
    square = u * u
    cube = square * u
    rest = 1.0 - u
    return (
        rest * rest * rest * (1.0 / 6.0),
        (3.0 * cube - 6.0 * square + 4.0) * (1.0 / 6.0),
        (-3.0 * cube + 3.0 * square + 3.0 * u + 1.0) * (1.0 / 6.0),
        cube * (1.0 / 6.0),
    )


def prepare(frac_ref, knot_ref, patt_ref, place_ref, high_ref, picks_ref):
    knot = knot_ref[...]
    high = (knot * 205) >> 10
    place_ref[...] = (knot - 5 * high + 1).astype(F32) + frac_ref[...]
    high_ref[...] = high.astype(F32)
    lane = lax.broadcasted_iota(I32, (8, 128), 1)
    picks = [jnp.where(lane == patt_ref[:, t : t + 1], 1.0, 0.0) for t in range(TILES_DEV)]
    picks_ref[...] = jnp.transpose(jnp.concatenate(picks, axis=0))[0:TD, :].astype(BF16)


def spreading(spread_ref):
    source = lax.broadcasted_iota(I32, (256, 256), 0)
    column = lax.broadcasted_iota(I32, (256, 256), 1)
    knot = jnp.where(column >= 128, 128 + (column & 31), column)
    spread_ref[...] = jnp.where(5 * (source & 31) + (source >> 5) == knot, 1.0, 0.0).astype(BF16)


def transposed(geom_ref, place_ref, high_ref, picks_ref, spread_ref, shape_ref, resid_ref, total, out_ref, parts_ref):
    places = lax.broadcasted_iota(I32, (8, 128), 0).astype(F32)
    rows = lax.broadcasted_iota(I32, (2, 16, 128), 0) * 16 + lax.broadcasted_iota(I32, (2, 16, 128), 1)
    rows = rows.astype(F32).astype(BF16)
    one, zero = jnp.ones((), BF16), jnp.zeros((), BF16)
    empty = jnp.zeros((16, 128), BF16)

    def tile(t):
        lanes = pl.ds(pl.multiple_of(t * 128, 128), 128)
        resid = jnp.broadcast_to(resid_ref[pl.ds(t, 1), :], (8, 128)) * (1.0 / 6.0)
        for pair in range(4):
            values, hits = [], []
            for half in range(2):
                s = slice(2 * pair + half, 2 * pair + half + 1)
                kept = pl.ds(pl.multiple_of((t * 8 + 2 * pair + half) * 8, 8), 8)
                if place_ref is None:
                    spline = shape_ref[kept, :]
                else:
                    near = jnp.abs(jnp.broadcast_to(place_ref[s, lanes], (8, 128)) - places)
                    a = jnp.maximum(2.0 - near, 0.0)
                    b = jnp.maximum(1.0 - near, 0.0)
                    spline = a * a * a - (4.0 * b) * (b * b)
                    shape_ref[kept, :] = spline
                value = jnp.broadcast_to(geom_ref[s, lanes], (8, 128)) * resid * spline
                rounded = value.astype(BF16).astype(F32)
                values.append(jnp.concatenate([rounded, value - rounded], axis=0).astype(BF16))
                at = jnp.broadcast_to(high_ref[s, lanes], (16, 128)).astype(BF16)
                hits.append(jnp.where(rows == at[None], one, zero).reshape(32, 128))
            left = jnp.concatenate(
                [jnp.concatenate([values[0], empty], axis=1), jnp.concatenate([empty, values[1]], axis=1)], axis=0
            )
            got = lax.dot_general(
                left, jnp.concatenate(hits, axis=1), (((1,), (1,)), ((), ())), preferred_element_type=F32
            )
            at = pl.ds(pl.multiple_of((t * 4 + pair) * 16, 16), 16)
            parts_ref[at, 0:32] = jnp.concatenate([got[0:8] + got[8:16], got[16:24] + got[24:32]], axis=0)

    def tiles(step, _):
        for at in range(UNROLL):
            tile(step * UNROLL + at)
        return 0

    lax.fori_loop(0, TILES_DEV // UNROLL, tiles, 0)

    picks = picks_ref[...]
    block = lax.broadcasted_iota(I32, (PAIRS, 128), 1) >> 5
    halves = []
    for group in range(2):
        piece = parts_ref[pl.ds(4 * group, PAIRS, stride=8), :]
        for q in range(1, 4):
            other = pltpu.roll(parts_ref[pl.ds(4 * group + q, PAIRS, stride=8), :], 32 * q, 1)
            piece = jnp.where(block >= q, other, piece)
        halves.append(piece)
    high, low = split(jnp.concatenate(halves, axis=1))
    grad = jnp.dot(picks, high, preferred_element_type=F32) + jnp.dot(picks, low, preferred_element_type=F32)
    spread = spread_ref[...]
    high, low = split(grad)
    grad = jnp.dot(high, spread, preferred_element_type=F32) + jnp.dot(low, spread, preferred_element_type=F32)
    out_ref[0:TD, :] = grad[:, 0:128]
    packed = grad[0:HIGH, 128:256]
    for q in range(1, 4):
        packed = jnp.where(block[0:HIGH] >= q, grad[q * HIGH : (q + 1) * HIGH, 128:256], packed)
    out_ref[TD:KNOTS, :] = packed
    sub = lax.broadcasted_iota(I32, (8, 128), 0)
    out_ref[KNOTS:TABLE, :] = jnp.where(sub == 0, total, 0.0)


def choose(patt_ref, picks_ref):
    lane = lax.broadcasted_iota(I32, (8, 128), 1)
    rows = [jnp.where(lane == patt_ref[:, t : t + 1], 1.0, 0.0) for t in range(TILES_DEV)]
    picks_ref[...] = jnp.concatenate(rows, axis=0).astype(BF16)


def applied(geom_ref, frac_ref, knot_ref, picks_ref, table, out_ref):
    packed = table[TD:KNOTS]
    tops = [packed] + [pltpu.roll(packed, 128 - 32 * q, 1) for q in range(1, 4)]
    tops = jnp.concatenate(tops + [jnp.zeros((TABLE - TD, 128), F32)], axis=0)
    both = jnp.concatenate([*split(table), *split(tops)], axis=1)
    gamma = jnp.broadcast_to(total_of(table[0:KNOTS] * table[0:KNOTS]), (8, 128))
    for c in range(out_ref.shape[0] // IMAGE):
        out_ref[c * IMAGE + 32 : (c + 1) * IMAGE, :] = gamma
    for t in range(TILES_DEV):
        if t % GROUP == 0:
            got = jnp.dot(picks_ref[8 * t : 8 * (t + GROUP), :], both, preferred_element_type=F32)
            bottoms = got[:, 0:128] + got[:, 128:256]
            uppers = got[:, 256:384] + got[:, 384:512]
        lanes = slice(128 * t, 128 * (t + 1))
        slots = slice(8 * (t % GROUP), 8 * (t % GROUP) + 8)
        base = knot_ref[:, lanes]
        value = None
        for j, weight in enumerate(weights(frac_ref[:, lanes])):
            at = (base + j) & 127
            near = jnp.take_along_axis(bottoms[slots], at, axis=1, mode="promise_in_bounds")
            far = jnp.take_along_axis(uppers[slots], at, axis=1, mode="promise_in_bounds")
            term = weight * jnp.where(base >= 128 - j, far, near)
            value = term if j == 0 else value + term
        row = jnp.sum(geom_ref[:, lanes] * value, axis=0, keepdims=True)
        for c in range(out_ref.shape[0] // IMAGE):
            out_ref[c * IMAGE + t : c * IMAGE + t + 1, :] = row


def first_back(*refs):
    sources, (out, *copies), (high, picks, spread, splines) = refs[:5], refs[5:11], refs[11:15]
    place, parts, sems = refs[15:]
    moves = [pltpu.make_async_copy(a, b, sems.at[i]) for i, (a, b) in enumerate(zip(sources, copies, strict=True))]
    for move in moves:
        move.start()
    spreading(spread)
    for move in moves:
        move.wait()
    geom, frac, knot, patt, target = copies
    prepare(frac, knot, patt, place, high, picks)
    transposed(geom, place, high, picks, spread, splines, target, 0.0, out, parts)


def later_back(geom, high, picks, spread, splines, got, out, image, gamma, parts):
    whole = parts_sum(got, got.shape[0] // IMAGE, IMAGE)
    image[...] = whole[0:32]
    gamma[...] = whole[32:40]
    total = jnp.broadcast_to(total_of(whole[0:32] * whole[0:32]), (8, 128))
    transposed(geom, None, high, picks, spread, splines, image, total, out, parts)


def scattered(count, groups, copies, got, out):
    rows = got.shape[0] // count
    for group in range(groups):
        total = got[group * rows : (group + 1) * rows, :]
        for at in range(group + groups, count, groups):
            total = total + got[at * rows : (at + 1) * rows, :]
        for at in range(copies):
            out[(at * groups + group) * rows : (at * groups + group + 1) * rows, :] = total


def first_forward(geom, frac, knot, patt, grad, out, picks):
    choose(patt, picks)
    applied(geom, frac, knot, picks, grad[...], out)


def later_forward(geom, frac, knot, picks, grad, other, gamma, out, table):
    alpha = gamma[0:1, :] / other[KNOTS : KNOTS + 1, :]
    table[...] = grad[...] - alpha * other[...]
    applied(geom, frac, knot, picks, table[...], out)


def norm_kernel(got, gamma, image, out, image_out, gamma_out):
    whole = parts_sum(got, got.shape[0] // IMAGE, IMAGE)
    gamma_out[...] = whole[32:40]
    beta = whole[32:33] / gamma[0:1, :]
    result = whole[0:32] + beta * image[...]
    image_out[...] = result
    out[...] = jnp.broadcast_to(total_of(result * result), out.shape)


def last_kernel(got, gamma0, gamma1, grad0, other, grad1, image0, image1, target, sol, resid):
    total1 = jnp.sum(got[...], axis=0, keepdims=True)
    alpha0 = gamma0[0:1, :] / other[KNOTS : KNOTS + 1, :]
    alpha1 = gamma1[0:1, :] / total1
    beta = gamma1[0:1, :] / gamma0[0:1, :]
    resid[...] = target[...] - alpha0 * image0[...] - alpha1 * image1[...]
    table = alpha0 * grad0[...] + alpha1 * (grad1[...] + beta * grad0[...])
    turned = jnp.transpose(table)
    sol[0:128, :] = turned[:, 0:TD]
    lane = lax.broadcasted_iota(I32, (32, 128), 1)
    top = pltpu.roll(turned[0:32], 128 - TD, 1)
    for q in range(1, 4):
        piece = pltpu.roll(turned[32 * q : 32 * q + 32], (128 - TD + HIGH * q) % 128, 1)
        top = jnp.where(lane >= HIGH * q, piece, top)
    sol[128:NK, :] = top[:, 0:TD]


def exchange(value, axis, count):
    rows = value.shape[0]
    got = lax.all_to_all(value.reshape(count, rows * 128 // count), axis, 0, 0, tiled=True)
    return got.reshape(rows, 128)


def on_device(geometry, fraction, interval, pattern, target):
    near = lax.axis_size("near")
    frames, doms, coefs = lax.axis_size("far") * near, lax.axis_size("dom"), lax.axis_size("coef")
    shape = jax.ShapeDtypeStruct
    parts = pltpu.VMEM((8 * PAIRS, 128), F32)

    def reduced(local):
        got = exchange(local, ("dom", "near"), doms * near)
        mine = frames * TABLE // (doms * near)
        (mine,) = call(functools.partial(scattered, doms * near, 1, frames), "scatter_dom", [(mine, 128)], [got])
        got = exchange(mine, ("far", "near"), frames)
        (mine,) = call(functools.partial(scattered, frames, near, doms), "scatter_frame", [(TABLE, 128)], [got])
        return exchange(mine, "dom", doms)

    sources = [geometry, fraction, interval, pattern, target.reshape(32, 128)]
    copies = [shape(s.shape, s.dtype) for s in sources]
    sources = [pltpu.with_memory_space_constraint(s, pltpu.HBM) for s in sources]
    local, geom, frac, knot, patt, target, high, types, spread, splines = call(
        first_back,
        "back0",
        [(TABLE, 128), *copies, (8, 4096), shape((TD, PAIRS), BF16), shape((256, 256), BF16), (8 * PAIRS, 128)],
        sources,
        [pltpu.VMEM((8, 4096), F32), parts, pltpu.SemaphoreType.DMA((5,))],
        HBM,
    )
    grad0 = reduced(local)
    local, picks = call(
        first_forward,
        "fwd0",
        [(coefs * IMAGE, 128), shape((PAIRS, 128), BF16)],
        [geom, frac, knot, patt, grad0],
    )
    got = exchange(local, "coef", coefs)
    local, image0, gamma0 = call(
        later_back, "back1", [(TABLE, 128), (32, 128), (8, 128)], [geom, high, types, spread, splines, got], [parts]
    )
    other = reduced(local)
    local, grad1 = call(
        later_forward,
        "fwd1",
        [(coefs * IMAGE, 128), (TABLE, 128)],
        [geom, frac, knot, picks, grad0, other, gamma0],
    )
    got = exchange(local, "coef", coefs)
    local, image1, gamma1 = call(
        norm_kernel, "norm", [(frames * doms, 128), (32, 128), (8, 128)], [got, gamma0, image0]
    )
    got = exchange(local, ("far", "near", "dom"), frames * doms)
    sol, resid = call(
        last_kernel,
        "last",
        [(NK, TD), (32, 128)],
        [got, gamma0, gamma1, grad0, other, grad1, image0, image1, target],
    )
    return sol.T, resid.reshape(4096)


def solution(mesh):
    frames, doms, coefs = mesh.devices.shape
    near = 2 if frames % 2 == 0 else 1
    mesh = jax.sharding.Mesh(mesh.devices.reshape(frames // near, near, doms, coefs), ("far", "near", "dom", "coef"))
    rows = ("far", "near", "dom")
    in_specs = (P("coef", rows), P("coef", rows), P("coef", rows), P("coef", rows), P(rows))
    out_specs = (P("coef", None), P(rows))
    return jax.shard_map(on_device, mesh=mesh, in_specs=in_specs, out_specs=out_specs, check_vma=False)
```

```python
import functools

import jax
import jax.numpy as jnp
from jax import lax
from jax.experimental import pallas as pl
from jax.experimental.pallas import tpu as pltpu
from jax.sharding import PartitionSpec as P

NK = 160
TYPES = 384
TD = 96
HIGH = 24
KNOTS = TD + HIGH
TABLE = 128
PAIRS = 256
IMAGE = 40
UNROLL = 16
GROUP = 8
TILES_DEV = 32

VMEM = pl.BlockSpec(memory_space=pltpu.VMEM)
HBM = pl.BlockSpec(memory_space=pltpu.HBM)
F32 = jnp.float32
BF16 = jnp.bfloat16
I32 = jnp.int32


def call(kernel, name, outs, args, scratch=(), space=VMEM):
    outs = [o if isinstance(o, jax.ShapeDtypeStruct) else jax.ShapeDtypeStruct(o, F32) for o in outs]
    return pl.pallas_call(
        kernel,
        out_shape=outs,
        in_specs=[space] * len(args),
        out_specs=[VMEM] * len(outs),
        scratch_shapes=list(scratch),
        name=name,
        compiler_params=pltpu.CompilerParams(vmem_limit_bytes=8 << 20),
    )(*args)


def split(value):
    high = value.astype(BF16)
    return high, (value - high.astype(F32)).astype(BF16)


def total_of(value):
    return jnp.sum(jnp.sum(value, axis=0, keepdims=True), axis=1, keepdims=True)


def parts_sum(ref, count, rows):
    total = ref[0:rows, :]
    for at in range(1, count):
        total = total + ref[at * rows : (at + 1) * rows, :]
    return total


def weights(u):
    square = u * u
    cube = square * u
    rest = 1.0 - u
    return (
        rest * rest * rest * (1.0 / 6.0),
        (3.0 * cube - 6.0 * square + 4.0) * (1.0 / 6.0),
        (-3.0 * cube + 3.0 * square + 3.0 * u + 1.0) * (1.0 / 6.0),
        cube * (1.0 / 6.0),
    )


def prepare(frac_ref, knot_ref, patt_ref, place_ref, high_ref, picks_ref):
    knot = knot_ref[...]
    high = (knot * 205) >> 10
    place_ref[...] = (knot - 5 * high + 1).astype(F32) + frac_ref[...]
    high_ref[...] = high.astype(F32)
    lane = lax.broadcasted_iota(I32, (8, 128), 1)
    picks = [jnp.where(lane == patt_ref[:, t : t + 1], 1.0, 0.0) for t in range(TILES_DEV)]
    picks_ref[...] = jnp.transpose(jnp.concatenate(picks, axis=0))[0:TD, :].astype(BF16)


def spreading(spread_ref):
    source = lax.broadcasted_iota(I32, (256, 256), 0)
    column = lax.broadcasted_iota(I32, (256, 256), 1)
    knot = jnp.where(column >= 128, 128 + (column & 31), column)
    spread_ref[...] = jnp.where(5 * (source & 31) + (source >> 5) == knot, 1.0, 0.0).astype(BF16)


def transposed(geom_ref, place_ref, high_ref, picks_ref, spread_ref, shape_ref, resid_ref, total, out_ref, parts_ref):
    places = lax.broadcasted_iota(I32, (8, 128), 0).astype(F32)
    rows = lax.broadcasted_iota(I32, (2, 16, 128), 0) * 16 + lax.broadcasted_iota(I32, (2, 16, 128), 1)
    rows = rows.astype(F32).astype(BF16)
    one, zero = jnp.ones((), BF16), jnp.zeros((), BF16)
    empty = jnp.zeros((16, 128), BF16)

    def tile(t):
        lanes = pl.ds(pl.multiple_of(t * 128, 128), 128)
        resid = jnp.broadcast_to(resid_ref[pl.ds(t, 1), :], (8, 128)) * (1.0 / 6.0)
        for pair in range(4):
            values, hits = [], []
            for half in range(2):
                s = slice(2 * pair + half, 2 * pair + half + 1)
                kept = pl.ds(pl.multiple_of((t * 8 + 2 * pair + half) * 8, 8), 8)
                if place_ref is None:
                    spline = shape_ref[kept, :]
                else:
                    near = jnp.abs(jnp.broadcast_to(place_ref[s, lanes], (8, 128)) - places)
                    a = jnp.maximum(2.0 - near, 0.0)
                    b = jnp.maximum(1.0 - near, 0.0)
                    spline = a * a * a - (4.0 * b) * (b * b)
                    shape_ref[kept, :] = spline
                value = jnp.broadcast_to(geom_ref[s, lanes], (8, 128)) * resid * spline
                rounded = value.astype(BF16).astype(F32)
                values.append(jnp.concatenate([rounded, value - rounded], axis=0).astype(BF16))
                at = jnp.broadcast_to(high_ref[s, lanes], (16, 128)).astype(BF16)
                hits.append(jnp.where(rows == at[None], one, zero).reshape(32, 128))
            left = jnp.concatenate(
                [jnp.concatenate([values[0], empty], axis=1), jnp.concatenate([empty, values[1]], axis=1)], axis=0
            )
            got = lax.dot_general(
                left, jnp.concatenate(hits, axis=1), (((1,), (1,)), ((), ())), preferred_element_type=F32
            )
            at = pl.ds(pl.multiple_of((t * 4 + pair) * 16, 16), 16)
            parts_ref[at, 0:32] = jnp.concatenate([got[0:8] + got[8:16], got[16:24] + got[24:32]], axis=0)

    def tiles(step, _):
        for at in range(UNROLL):
            tile(step * UNROLL + at)
        return 0

    lax.fori_loop(0, TILES_DEV // UNROLL, tiles, 0)

    picks = picks_ref[...]
    block = lax.broadcasted_iota(I32, (PAIRS, 128), 1) >> 5
    halves = []
    for group in range(2):
        piece = parts_ref[pl.ds(4 * group, PAIRS, stride=8), :]
        for q in range(1, 4):
            other = pltpu.roll(parts_ref[pl.ds(4 * group + q, PAIRS, stride=8), :], 32 * q, 1)
            piece = jnp.where(block >= q, other, piece)
        halves.append(piece)
    high, low = split(jnp.concatenate(halves, axis=1))
    grad = jnp.dot(picks, high, preferred_element_type=F32) + jnp.dot(picks, low, preferred_element_type=F32)
    spread = spread_ref[...]
    high, low = split(grad)
    grad = jnp.dot(high, spread, preferred_element_type=F32) + jnp.dot(low, spread, preferred_element_type=F32)
    out_ref[0:TD, :] = grad[:, 0:128]
    packed = grad[0:HIGH, 128:256]
    for q in range(1, 4):
        packed = jnp.where(block[0:HIGH] >= q, grad[q * HIGH : (q + 1) * HIGH, 128:256], packed)
    out_ref[TD:KNOTS, :] = packed
    sub = lax.broadcasted_iota(I32, (8, 128), 0)
    out_ref[KNOTS:TABLE, :] = jnp.where(sub == 0, total, 0.0)


def choose(patt_ref, picks_ref):
    lane = lax.broadcasted_iota(I32, (8, 128), 1)
    rows = [jnp.where(lane == patt_ref[:, t : t + 1], 1.0, 0.0) for t in range(TILES_DEV)]
    picks_ref[...] = jnp.concatenate(rows, axis=0).astype(BF16)


def applied(geom_ref, frac_ref, knot_ref, picks_ref, table, out_ref):
    packed = table[TD:KNOTS]
    tops = [packed] + [pltpu.roll(packed, 128 - 32 * q, 1) for q in range(1, 4)]
    tops = jnp.concatenate(tops + [jnp.zeros((TABLE - TD, 128), F32)], axis=0)
    both = jnp.concatenate([*split(table), *split(tops)], axis=1)
    gamma = jnp.broadcast_to(total_of(table[0:KNOTS] * table[0:KNOTS]), (8, 128))
    for c in range(out_ref.shape[0] // IMAGE):
        out_ref[c * IMAGE + 32 : (c + 1) * IMAGE, :] = gamma
    for t in range(TILES_DEV):
        if t % GROUP == 0:
            got = jnp.dot(picks_ref[8 * t : 8 * (t + GROUP), :], both, preferred_element_type=F32)
            bottoms = got[:, 0:128] + got[:, 128:256]
            uppers = got[:, 256:384] + got[:, 384:512]
        lanes = slice(128 * t, 128 * (t + 1))
        slots = slice(8 * (t % GROUP), 8 * (t % GROUP) + 8)
        base = knot_ref[:, lanes]
        value = None
        for j, weight in enumerate(weights(frac_ref[:, lanes])):
            at = (base + j) & 127
            near = jnp.take_along_axis(bottoms[slots], at, axis=1, mode="promise_in_bounds")
            far = jnp.take_along_axis(uppers[slots], at, axis=1, mode="promise_in_bounds")
            term = weight * jnp.where(base >= 128 - j, far, near)
            value = term if j == 0 else value + term
        row = jnp.sum(geom_ref[:, lanes] * value, axis=0, keepdims=True)
        for c in range(out_ref.shape[0] // IMAGE):
            out_ref[c * IMAGE + t : c * IMAGE + t + 1, :] = row


def first_back(*refs):
    sources, (out, *copies), (high, picks, spread, splines) = refs[:5], refs[5:11], refs[11:15]
    place, parts, sems = refs[15:]
    moves = [pltpu.make_async_copy(a, b, sems.at[i]) for i, (a, b) in enumerate(zip(sources, copies, strict=True))]
    for at in (1, 2, 3, 0, 4):
        moves[at].start()
    spreading(spread)
    geom, frac, knot, patt, target = copies
    for at in (1, 2, 3):
        moves[at].wait()
    prepare(frac, knot, patt, place, high, picks)
    for at in (0, 4):
        moves[at].wait()
    transposed(geom, place, high, picks, spread, splines, target, 0.0, out, parts)


def later_back(geom, high, picks, spread, splines, got, out, image, gamma, parts):
    whole = parts_sum(got, got.shape[0] // IMAGE, IMAGE)
    image[...] = whole[0:32]
    gamma[...] = whole[32:40]
    total = jnp.broadcast_to(total_of(whole[0:32] * whole[0:32]), (8, 128))
    transposed(geom, None, high, picks, spread, splines, image, total, out, parts)


def scattered(count, groups, copies, got, out):
    rows = got.shape[0] // count
    for group in range(groups):
        total = got[group * rows : (group + 1) * rows, :]
        for at in range(group + groups, count, groups):
            total = total + got[at * rows : (at + 1) * rows, :]
        for at in range(copies):
            out[(at * groups + group) * rows : (at * groups + group + 1) * rows, :] = total


def first_forward(geom, frac, knot, patt, grad, out, picks):
    choose(patt, picks)
    applied(geom, frac, knot, picks, grad[...], out)


def later_forward(geom, frac, knot, picks, grad, other, gamma, out, table):
    alpha = gamma[0:1, :] / other[KNOTS : KNOTS + 1, :]
    table[...] = grad[...] - alpha * other[...]
    applied(geom, frac, knot, picks, table[...], out)


def norm_kernel(got, gamma, image, out, image_out, gamma_out):
    whole = parts_sum(got, got.shape[0] // IMAGE, IMAGE)
    gamma_out[...] = whole[32:40]
    beta = whole[32:33] / gamma[0:1, :]
    result = whole[0:32] + beta * image[...]
    image_out[...] = result
    out[...] = jnp.broadcast_to(total_of(result * result), out.shape)


def last_kernel(got, gamma0, gamma1, grad0, other, grad1, image0, image1, target, sol, resid):
    total1 = jnp.sum(got[...], axis=0, keepdims=True)
    alpha0 = gamma0[0:1, :] / other[KNOTS : KNOTS + 1, :]
    alpha1 = gamma1[0:1, :] / total1
    beta = gamma1[0:1, :] / gamma0[0:1, :]
    resid[...] = target[...] - alpha0 * image0[...] - alpha1 * image1[...]
    table = alpha0 * grad0[...] + alpha1 * (grad1[...] + beta * grad0[...])
    turned = jnp.transpose(table)
    sol[0:128, :] = turned[:, 0:TD]
    lane = lax.broadcasted_iota(I32, (32, 128), 1)
    top = pltpu.roll(turned[0:32], 128 - TD, 1)
    for q in range(1, 4):
        piece = pltpu.roll(turned[32 * q : 32 * q + 32], (128 - TD + HIGH * q) % 128, 1)
        top = jnp.where(lane >= HIGH * q, piece, top)
    sol[128:NK, :] = top[:, 0:TD]


def exchange(value, axis, count):
    rows = value.shape[0]
    got = lax.all_to_all(value.reshape(count, rows * 128 // count), axis, 0, 0, tiled=True)
    return got.reshape(rows, 128)


def on_device(geometry, fraction, interval, pattern, target):
    near = lax.axis_size("near")
    frames, doms, coefs = lax.axis_size("far") * near, lax.axis_size("dom"), lax.axis_size("coef")
    shape = jax.ShapeDtypeStruct
    parts = pltpu.VMEM((8 * PAIRS, 128), F32)

    def reduced(local):
        got = exchange(local, ("dom", "near"), doms * near)
        mine = frames * TABLE // (doms * near)
        (mine,) = call(functools.partial(scattered, doms * near, 1, frames), "scatter_dom", [(mine, 128)], [got])
        got = exchange(mine, ("far", "near"), frames)
        (mine,) = call(functools.partial(scattered, frames, near, doms), "scatter_frame", [(TABLE, 128)], [got])
        return exchange(mine, "dom", doms)

    sources = [geometry, fraction, interval, pattern, target.reshape(32, 128)]
    copies = [shape(s.shape, s.dtype) for s in sources]
    sources = [pltpu.with_memory_space_constraint(s, pltpu.HBM) for s in sources]
    local, geom, frac, knot, patt, target, high, types, spread, splines = call(
        first_back,
        "back0",
        [(TABLE, 128), *copies, (8, 4096), shape((TD, PAIRS), BF16), shape((256, 256), BF16), (8 * PAIRS, 128)],
        sources,
        [pltpu.VMEM((8, 4096), F32), parts, pltpu.SemaphoreType.DMA((5,))],
        HBM,
    )
    grad0 = reduced(local)
    local, picks = call(
        first_forward,
        "fwd0",
        [(coefs * IMAGE, 128), shape((PAIRS, 128), BF16)],
        [geom, frac, knot, patt, grad0],
    )
    got = exchange(local, "coef", coefs)
    local, image0, gamma0 = call(
        later_back, "back1", [(TABLE, 128), (32, 128), (8, 128)], [geom, high, types, spread, splines, got], [parts]
    )
    other = reduced(local)
    local, grad1 = call(
        later_forward,
        "fwd1",
        [(coefs * IMAGE, 128), (TABLE, 128)],
        [geom, frac, knot, picks, grad0, other, gamma0],
    )
    got = exchange(local, "coef", coefs)
    local, image1, gamma1 = call(
        norm_kernel, "norm", [(frames * doms, 128), (32, 128), (8, 128)], [got, gamma0, image0]
    )
    got = exchange(local, ("far", "near", "dom"), frames * doms)
    sol, resid = call(
        last_kernel,
        "last",
        [(NK, TD), (32, 128)],
        [got, gamma0, gamma1, grad0, other, grad1, image0, image1, target],
    )
    return sol.T, resid.reshape(4096)


def solution(mesh):
    frames, doms, coefs = mesh.devices.shape
    near = 2 if frames % 2 == 0 else 1
    mesh = jax.sharding.Mesh(mesh.devices.reshape(frames // near, near, doms, coefs), ("far", "near", "dom", "coef"))
    rows = ("far", "near", "dom")
    in_specs = (P("coef", rows), P("coef", rows), P("coef", rows), P("coef", rows), P(rows))
    out_specs = (P("coef", None), P(rows))
    return jax.shard_map(on_device, mesh=mesh, in_specs=in_specs, out_specs=out_specs, check_vma=False)
```
